32 devices in a mesh: section: 4 (over x, core), dp: 8 (over z, y).
Axes of the slice: x: 2, y: 2, z: 4, core: 2. Of those that a mesh axis runs over, the one named last changes fastest.
Arguments:
- token_ids: int32 [2, 16], P(None, 'dp'), may hold values from 0 to 8191
- target_ids: int32 [2, 16], P(None, 'dp'), may hold values from 0 to 8191
- table: bfloat16 [8192, 4608], P(('section', 'dp')), may hold values from -0.06629126 to 0.06629126
- norm_gain: bfloat16 [2, 4, 4608], P(None, 'section'), may hold values from 0.099609375 to 1.8984375
- w_in: bfloat16 [2, 4, 8, 4608], P(None, 'section'), may hold values from -0.09375 to 0.09375
- w_out: bfloat16 [2, 4, 8, 4608], P(None, 'section'), may hold values from -2 to 2
- final_gain: bfloat16 [4608], replicated, may hold values from 0.099609375 to 1.8984375
Outputs:
- token_loss: float32 [2, 16], P(None, 'dp')
- table_grad: bfloat16 [8192, 4608], P(('section', 'dp'))
The draws below stay inside these ranges and needn't reach their ends.
All inputs are finite; a program needn't handle non-finite values.
Results may differ from the reference program's by a relative error of at most 0.013.
The reference program's roundings to bfloat16 on the way (of `embedded`, `final_rows`, `head_input`, `score_grad`, `final_grad` and `embedded_grad`) count: a program that leaves them out, or rounds other values in their place, can miss the bound.
Values may be sent and summed in bfloat16 or wider, within the bound.
A program may use at most 64 MiB of HBM per device.

```python
import math
import jax
import jax.numpy as jnp
import numpy as np
from jax import lax

D = 4608
RANK = 8
V_DEV = 256
M = 2
VOCAB = 8192
TOKENS = 16
N_SECTION = 4


def draw_table(key, part):
    direction_key, level_key, jitter_key, noise_key = jax.random.split(key, 4)
    row_scale = 0.55 / D ** 0.5
    regions = VOCAB // V_DEV
    direction = jnp.clip(jax.random.normal(direction_key, (D,), jnp.float32), -2.5, 2.5)
    levels = jax.random.uniform(level_key, (regions,), jnp.float32, 0.5, 1.5)
    noise_part = jnp.clip(jax.random.normal(noise_key, (VOCAB, D), jnp.float32), -3.5, 3.5)
    jitter = jax.random.uniform(jitter_key, (VOCAB,), jnp.float32, 0.8, 1.2)
    loading = jnp.broadcast_to(levels[:, None], (regions, V_DEV)).reshape(VOCAB) * jitter
    return (row_scale * (loading[:, None] * direction[None, :] + noise_part)).astype(jnp.bfloat16)


def place_ends(array, stream_key, smallest, high):
    dims = array.shape
    index_at = [jax.random.randint(jax.random.fold_in(stream_key, axis), (), 0, dims[axis]) for axis in range(len(dims))]
    array = array.at[tuple(index_at)].set(smallest)
    longest = dims.index(max(dims))
    index_at[longest] = (index_at[longest] + 1) % dims[longest]
    return array.at[tuple(index_at)].set(high)


def block_levels(rng, dims, pieces, least, top_value):
    level, own = 1.0, jax.random.fold_in(rng, 6)
    for axis_at, shards_of in pieces:
        draws = jnp.exp(jax.random.uniform(jax.random.fold_in(own, axis_at), (shards_of,), jnp.float32, least / len(pieces), top_value / len(pieces)))
        level = level * jnp.repeat(draws, dims[axis_at] // shards_of).reshape([-1 if axis == axis_at else 1 for axis in range(len(dims))])
    return level


def rank_bounds(count, slope):
    loads = [(1 << 20) // math.isqrt(rank ** slope) + 1 for rank in range(1, count + 1)]
    deviation = 1 + sum(loads) // (1 << 30)
    return np.cumsum(np.array([max(1, weight // deviation) for weight in loads]))


def ranked(rng, dims, number_of, lean):
    grid = rank_bounds(number_of, lean)
    pick = jax.random.randint(jax.random.fold_in(rng, 1), dims, 0, int(grid[number_of - 1]))
    grade = jnp.searchsorted(jnp.asarray(grid, jnp.int32), pick, side="right")
    return jax.random.permutation(jax.random.fold_in(rng, 2), number_of)[grade].astype(jnp.int32)


def gaussian(key, extent, scale, most, cuts=(), kind=jnp.bfloat16):
    drawn = scale * jax.random.normal(key, extent, jnp.float32)
    if cuts:
        drawn = drawn * block_levels(key, extent, cuts, -0.22, 0.18)
    return jnp.clip(drawn, -most, most).astype(kind)


def setup_inputs(seed: int = 0) -> dict:
    keys = jax.random.split(jax.random.key(seed), 8)
    token_ids = place_ends(ranked(keys[0], (M, TOKENS), VOCAB, 2), jax.random.fold_in(keys[0], 3), 0, VOCAB - 1).astype(jnp.int32)
    target_ids = place_ends(ranked(keys[1], (M, TOKENS), VOCAB, 2), jax.random.fold_in(keys[1], 3), 0, VOCAB - 1).astype(jnp.int32)
    table = draw_table(jax.random.fold_in(keys[7], 71), 0)
    norm_gain = jnp.clip(1.0 + 0.18 * jax.random.normal(keys[3], (2, N_SECTION, D), jnp.float32), 0.099609375, 1.8984375).astype(jnp.bfloat16)
    w_in = gaussian(keys[4], (2, N_SECTION, RANK, D), D ** -0.5, 0.09375, ((1, 4),))
    w_out = gaussian(keys[5], (2, N_SECTION, RANK, D), RANK ** -0.5, 2.0, ((1, 4),))
    final_gain = jnp.clip(1.0 + 0.18 * jax.random.normal(keys[6], (D,), jnp.float32), 0.099609375, 1.8984375).astype(jnp.bfloat16)
    return dict(token_ids=token_ids, target_ids=target_ids, table=table, norm_gain=norm_gain, w_in=w_in, w_out=w_out, final_gain=final_gain)


EPS = 1e-06
CAP = 30.0
GELU_C = 0.7978845608028654

def gelu_tanh(values):
    return 0.5 * values * (1.0 + jnp.tanh(GELU_C * (values + 0.044715 * values * values * values)))

def gelu_slope(values):
    inner = jnp.tanh(GELU_C * (values + 0.044715 * values * values * values))
    return 0.5 * (1.0 + inner) + 0.5 * values * (1.0 - inner * inner) * GELU_C * (1.0 + 3.0 * 0.044715 * values * values)

def normalize(rows_in):
    values = rows_in.astype(jnp.float32)
    scale = lax.rsqrt(lax.optimization_barrier(jnp.mean(values * values, axis=-1, keepdims=True)) + EPS)
    return (values * scale, scale)

def norm_back(normed, scale, grad):
    return scale * (grad - normed * lax.optimization_barrier(jnp.mean(grad * normed, axis=-1, keepdims=True)))

def layer_forward(rows_in, gain, first_proj, second_proj):
    normed, scale = normalize(rows_in)
    activated = (normed * gain.astype(jnp.float32)).astype(jnp.bfloat16)
    preact = lax.dot_general(activated, first_proj, (((1,), (1,)), ((), ())), preferred_element_type=jnp.float32)
    hidden = gelu_tanh(preact).astype(jnp.bfloat16)
    branch = jnp.dot(hidden, second_proj, preferred_element_type=jnp.float32)
    return (rows_in.astype(jnp.float32) + branch).astype(jnp.bfloat16)

def layer_backward(rows_in, gain, first_proj, second_proj, grad_out):
    normed, scale = normalize(rows_in)
    gain_float = gain.astype(jnp.float32)
    activated = (normed * gain_float).astype(jnp.bfloat16)
    preact = lax.dot_general(activated, first_proj, (((1,), (1,)), ((), ())), preferred_element_type=jnp.float32)
    hidden_grad = lax.dot_general(grad_out, second_proj, (((1,), (1,)), ((), ())), preferred_element_type=jnp.float32)
    preact_grad = (hidden_grad * gelu_slope(preact)).astype(jnp.bfloat16)
    act_grad = jnp.dot(preact_grad, first_proj, preferred_element_type=jnp.float32)
    return (grad_out.astype(jnp.float32) + norm_back(normed, scale, act_grad * gain_float)).astype(jnp.bfloat16)

def reference(token_ids, target_ids, table, norm_gain, w_in, w_out, final_gain):
    layer_total = 2 * N_SECTION
    layer_gains = norm_gain.reshape(layer_total, D)
    weights_in = w_in.reshape(layer_total, RANK, D)
    weights_out = w_out.reshape(layer_total, RANK, D)
    embed_scale = math.sqrt(D)
    final_scale = final_gain.astype(jnp.float32)
    vocab_index = jnp.arange(VOCAB, dtype=jnp.int32)

    def one_batch(carry, batch_item):
        input_list, goal_list = batch_item
        embedded = (table[input_list].astype(jnp.float32) * embed_scale).astype(jnp.bfloat16)

        def forward_layer(current, layer_params):
            gain, first_proj, second_proj = layer_params
            return (layer_forward(current, gain, first_proj, second_proj), current)
        final_rows, stored = lax.scan(forward_layer, embedded, (layer_gains, weights_in, weights_out))
        normed, scale = normalize(final_rows)
        head_input = (normed * final_scale).astype(jnp.bfloat16)
        scores = lax.dot_general(head_input, table, (((1,), (1,)), ((), ())), preferred_element_type=jnp.float32)
        squash = jnp.tanh(scores / CAP)
        capped = CAP * squash
        powers = jnp.exp(capped)
        exp_total = lax.optimization_barrier(jnp.sum(powers, axis=1))
        target_mask = goal_list[:, None] == vocab_index[None, :]
        target_score = lax.optimization_barrier(jnp.sum(jnp.where(target_mask, capped, jnp.float32(0.0)), axis=1))
        token_loss = jnp.log(exp_total) - target_score
        score_grad = ((powers / exp_total[:, None] - target_mask.astype(jnp.float32)) * (1.0 - squash * squash)).astype(jnp.bfloat16)
        head_input_grad = jnp.dot(score_grad, table, preferred_element_type=jnp.float32)
        final_grad = norm_back(normed, scale, head_input_grad * final_scale).astype(jnp.bfloat16)

        def backward_layer(grad_now, layer_params):
            rows_in, gain, first_proj, second_proj = layer_params
            return (layer_backward(rows_in, gain, first_proj, second_proj, grad_now), None)
        embedded_grad, _ = lax.scan(backward_layer, final_grad, (stored, layer_gains, weights_in, weights_out), reverse=True)
        return (carry, (token_loss, score_grad, head_input, embedded_grad))
    start = jnp.zeros((), jnp.float32)
    _, outputs = lax.scan(one_batch, start, (token_ids, target_ids))
    losses, score_grads, head_inputs, embedded_grads = outputs
    head_part = lax.dot_general(score_grads.reshape(-1, VOCAB), head_inputs.reshape(-1, D), (((0,), (0,)), ((), ())), preferred_element_type=jnp.float32)
    table_grad = head_part.at[token_ids.reshape(-1)].add(embedded_grads.reshape(-1, D).astype(jnp.float32) * embed_scale)
    return (losses, table_grad.astype(jnp.bfloat16))
```

```python
import functools
import math

import jax
import jax.numpy as jnp
import ml_dtypes
import numpy as np
from jax import lax
from jax.experimental import pallas as pl
from jax.experimental.pallas import tpu as pltpu
from jax.sharding import PartitionSpec as P

EPS = 1e-06
CAP = 30.0
GELU_C = 0.7978845608028654
LANES = 128
F32 = jnp.float32
BF16 = jnp.bfloat16
IDS, LOOK, HEAD, STAT, GRAD, EMB, GAIN, WIN, WOUT = range(9)
RELAY = 3
TABLE = 12
PAIR = 13
GOAL = 20
OUT = 34


def gelu_tanh(values):
    return 0.5 * values * (1.0 + jnp.tanh(GELU_C * (values + 0.044715 * values * values * values)))


def gelu_slope(values):
    inner = jnp.tanh(GELU_C * (values + 0.044715 * values * values * values))
    return 0.5 * (1.0 + inner) + 0.5 * values * (1.0 - inner * inner) * GELU_C * (
        1.0 + 3.0 * 0.044715 * values * values
    )


def rounded(values):
    return values.astype(BF16).astype(F32)


def cascade(
    sections, replicas, per_dp, pad,
    token_ref, target_ref, table_hbm, gain_ref, fgain_ref, win_ref, wout_ref,
    loss_ref, left_hbm, right_hbm,
    left_ref, right_ref, loss_all, ids_ref, idbuf, idrow, gains, wins, wouts, flat, look_out, look_in, tok, layer_in,
    head_out, head_in, stat_out, stat_in, grad_out, grad_in, emb_out, emb_in,
    table_ref, gain_wide, kept, look_pair, grad_pair, goal_out, goal_pair, goal_in, totals, send_sem, recv_sem,
):
    devices = sections * replicas
    tokens = replicas * per_dp
    rows_dev, dim = table_ref.shape
    chunks = dim // LANES
    head_ref = right_ref.at[pl.ds(0, tokens)]
    layers = 2 * sections
    scale_in = math.sqrt(dim)
    sec, rep = lax.axis_index("section"), lax.axis_index("dp")
    me = sec * replicas + rep
    offset = me * rows_dev
    all_own = per_dp == sections
    own = sec < per_dp
    own_half = per_dp // 2
    count_half = tokens // 2
    half = sections // 2
    side, partner = sec % 2, sec + 1 - 2 * (sec % 2)
    my_half = rep * own_half + sec // 2
    if not all_own:
        my_half = jnp.where(own, my_half, -1)

    def if_own(body):
        if all_own:
            body()
        else:
            pl.when(own)(body)

    def spread(phase, count, first, target, skip, src, dst):
        def step(i, _):
            at = lax.rem(first + i, count)

            @pl.when(at != skip)
            def _():
                pltpu.make_async_remote_copy(
                    src_ref=src(at),
                    dst_ref=dst,
                    send_sem=send_sem.at[phase],
                    recv_sem=recv_sem.at[phase],
                    device_id=target(at),
                    device_id_type=pl.DeviceIdType.MESH,
                ).start()

            @pl.when(at == skip)
            def _():
                pltpu.make_async_copy(src(at), dst, recv_sem.at[phase]).start()

            return 0

        lax.fori_loop(0, count, step, 0, unroll=8)

    def take(ref, sem):
        pltpu.make_async_copy(ref, ref, sem).wait()

    def any_device(n):
        return (n // replicas, n % replicas)

    def token_device(h):
        return (2 * (h % own_half) + side, h // own_half)

    def side_device(q):
        return (2 * (q // replicas) + side, q % replicas)

    side_me = (sec // 2) * replicas + rep

    def pair_copy(phase, src, dst):
        return pltpu.make_async_remote_copy(
            src_ref=src,
            dst_ref=dst,
            send_sem=send_sem.at[phase],
            recv_sem=recv_sem.at[phase],
            device_id=(partner, rep),
            device_id_type=pl.DeviceIdType.MESH,
        )

    load = pltpu.make_async_copy(table_hbm, table_ref, recv_sem.at[TABLE])
    load.start()
    barrier = pltpu.get_barrier_semaphore()

    def greet(i, _):
        n = lax.rem(me + 1 + i, devices)
        pl.semaphore_signal(
            barrier, inc=1, device_id=any_device(n), device_id_type=pl.DeviceIdType.MESH
        )
        return 0

    lax.fori_loop(0, devices - 1, greet, 0, unroll=8)
    flat[...] = jnp.zeros_like(flat)
    tok[...] = jnp.zeros_like(tok)
    row = lax.broadcasted_iota(jnp.int32, (2 * per_dp, LANES), 0)
    made = jnp.zeros((2 * per_dp, LANES), jnp.int32)
    batches, width = token_ref.shape
    for b in range(batches):
        for w in range(width):
            k = b * width + w
            made = jnp.where(row == k, token_ref[b : b + 1, w : w + 1], made)
            made = jnp.where(row == per_dp + k, target_ref[b : b + 1, w : w + 1], made)
    ids_ref[...] = made
    pl.semaphore_wait(barrier, devices - 1)

    spread(IDS, replicas, rep, lambda d: (sec, d), rep, lambda d: ids_ref, idbuf.at[rep])
    stores = ((GAIN, gain_ref, gains), (WIN, win_ref, wins), (WOUT, wout_ref, wouts))
    for phase, src, dst in stores:
        for i in range(1, half):
            pair = lax.rem(sec // 2 + i, half)
            pltpu.make_async_remote_copy(
                src_ref=src,
                dst_ref=dst.at[side, sec // 2],
                send_sem=send_sem.at[phase],
                recv_sem=recv_sem.at[phase],
                device_id=(2 * pair + side, rep),
                device_id_type=pl.DeviceIdType.MESH,
            ).start()
        pltpu.make_async_copy(src, dst.at[side, sec // 2], recv_sem.at[phase]).start()

    take(idbuf, recv_sem.at[IDS])
    for d in range(replicas):
        for kind in range(2):
            for k in range(per_dp):
                at = (k % 2) * count_half + d * own_half + k // 2
                idrow[kind, pl.ds(at, 1), :] = idbuf[
                    d, pl.ds(kind * per_dp + k, 1), :
                ]
    wide = lambda value: jnp.concatenate([value] * (rows_dev // LANES), axis=1)
    column = lax.broadcasted_iota(jnp.int32, (tokens, rows_dev), 1) + offset
    chosen = jnp.where(wide(idrow[0]) == column, 1.0, 0.0).astype(BF16)
    mask = wide(idrow[1]) == column
    high_scale = float(np.float32(scale_in).astype(ml_dtypes.bfloat16))
    low_scale = float(np.float32(scale_in - high_scale).astype(ml_dtypes.bfloat16))
    left_ref[pl.ds(tokens, tokens), :] = (chosen.astype(F32) * high_scale).astype(BF16)
    left_ref[pl.ds(2 * tokens, tokens), :] = (chosen.astype(F32) * low_scale).astype(BF16)
    load.wait()

    def scatter(left, phase, out, pair, into):
        for j in range(0, chunks, 2):
            part = jnp.dot(
                left, table_ref[:, j * LANES : (j + 2) * LANES], preferred_element_type=F32
            )
            flat[pl.ds(j, tokens, stride=pad), :] = part[:, :LANES]
            flat[pl.ds(j + 1, tokens, stride=pad), :] = part[:, LANES:]
        mine = pl.ds(pl.multiple_of(side * (count_half * pad), 8), count_half * pad)
        away = pl.ds(pl.multiple_of((1 - side) * (count_half * pad), 8), count_half * pad)
        blocks = (count_half, pad // 8, 8, LANES)
        out[1 - side] = flat[away, :].reshape(blocks).astype(BF16)
        swap = pair_copy(phase + PAIR, out.at[1 - side], pair)
        swap.start()
        swap.wait()
        out[side] = (flat[mine, :].reshape(blocks) + pair[...].astype(F32)).astype(BF16)
        spread(
            phase, count_half, rep * own_half + sec // 2, token_device, my_half,
            lambda h: out.at[side, h], into.at[side_me],
        )

    def total(into):
        return lax.fori_loop(
            0, devices // 2, lambda n, acc: acc + into[n].astype(F32),
            jnp.zeros((pad // 8, 8, LANES), F32),
            unroll=4,
        ).reshape(pad, LANES)

    def spread_rows(values):
        tok[...] = values
        return jnp.concatenate(
            [jnp.broadcast_to(tok[j : j + 1, :], (8, LANES)) for j in range(chunks)], axis=1
        )

    def pack_row(values, out):
        for j in range(chunks):
            tok[j : j + 1, :] = values[0:1, j * LANES : (j + 1) * LANES]
        out[...] = tok[...].reshape(pad // 8, 8, LANES).astype(BF16)

    def norm(x):
        scale = lax.rsqrt(jnp.sum(x * x, axis=1, keepdims=True) * (1.0 / dim) + EPS)
        return x * scale, scale

    def weights(layer):
        s, c = layer % sections, layer // sections
        at = (s % 2, s // 2, c, 0)
        return gain_wide[layer], wins[at].astype(F32), wouts[at].astype(F32)

    def widen(layer, _):
        s, c = layer % sections, layer // sections
        both = gains[s % 2, s // 2].astype(F32)
        picked = jnp.where(c == 0, both[0:1], both[1:2])
        gain_wide[layer] = jnp.broadcast_to(picked, (8, dim))
        return 0

    def gather(phase, block, into):
        if_own(
            lambda: spread(
                phase, devices // 2, side_me, side_device, side_me,
                lambda n: block, into.at[side, my_half],
            )
        )
        take(into.at[side], recv_sem.at[phase])
        relay = pair_copy(phase + PAIR, into.at[side], into.at[side])
        relay.start()
        relay.wait()

    def unpack(into, out):
        flat[...] = into[...].astype(F32).reshape(tokens * pad, LANES)
        for j in range(chunks):
            out(slice(j * LANES, (j + 1) * LANES), flat[pl.ds(j, tokens, stride=pad), :])

    scatter(chosen, LOOK, look_out, look_pair, look_in)
    scatter(jnp.where(mask, 1.0, 0.0).astype(BF16), GOAL, goal_out, goal_pair, goal_in)
    for phase, _, buf in stores:
        take(buf.at[side], recv_sem.at[phase])
        pltpu.make_async_remote_copy(
            src_ref=buf.at[side],
            dst_ref=buf.at[side],
            send_sem=send_sem.at[phase + RELAY],
            recv_sem=recv_sem.at[phase + RELAY],
            device_id=(partner, rep),
            device_id_type=pl.DeviceIdType.MESH,
        ).start()
    gain_wide[layers] = jnp.broadcast_to(fgain_ref[...].astype(F32)[None], (8, dim))
    take(gains.at[1 - side], recv_sem.at[GAIN + RELAY])
    lax.fori_loop(0, layers, widen, 0)
    for phase, _, buf in stores[1:]:
        take(buf.at[1 - side], recv_sem.at[phase + RELAY])

    def forward():
        take(look_in, recv_sem.at[LOOK])
        x = spread_rows(rounded(total(look_in) * scale_in))

        def layer(index, x):
            layer_in[index] = x
            gain, first, second = weights(index)
            normed, scale = norm(x)
            pre = jnp.sum(rounded(normed * gain) * first, axis=1, keepdims=True)
            hidden = rounded(gelu_tanh(pre))
            kept[index, 0] = jnp.broadcast_to(scale, (8, LANES))
            kept[index, 1] = jnp.broadcast_to(gelu_slope(pre), (8, LANES))
            return rounded(x + jnp.sum(hidden * second, axis=0, keepdims=True))

        x = lax.fori_loop(0, layers, layer, x, unroll=2)
        layer_in[layers] = x
        normed, _ = norm(x)
        pack_row(normed * gain_wide[layers], head_out)

    if_own(forward)
    gather(HEAD, head_out, head_in)

    def store_head(lanes, part):
        right_ref[pl.ds(0, tokens), lanes] = part.astype(BF16)

    unpack(head_in, store_head)

    scores = lax.dot_general(
        head_ref[...], table_ref[...], (((1,), (1,)), ((), ())), preferred_element_type=F32
    )
    squash = jnp.tanh(scores / CAP)
    capped = CAP * squash
    powers = jnp.exp(capped)
    slope = 1.0 - squash * squash
    others = jnp.where(mask, 0.0, powers)
    exp_sum = jnp.sum(others, axis=1, keepdims=True)
    goal = jnp.sum(jnp.where(mask, capped, 0.0), axis=1, keepdims=True)
    lane = lax.broadcasted_iota(jnp.int32, (tokens, LANES), 1)
    here = lane == lax.broadcasted_iota(jnp.int32, (tokens, LANES), 0)
    stat_out[0:1, :] = jnp.sum(jnp.where(here, exp_sum, 0.0), axis=0, keepdims=True)
    stat_out[1:2, :] = jnp.sum(jnp.where(here, goal, 0.0), axis=0, keepdims=True)
    spread(STAT, devices, me, any_device, me, lambda n: stat_out, stat_in.at[me])
    scatter((others * slope).astype(BF16), GRAD, grad_out, grad_pair, grad_in)
    take(stat_in, recv_sem.at[STAT])
    tile = lax.fori_loop(
        0, devices, lambda n, acc: acc + stat_in[n], jnp.zeros((2, LANES), F32), unroll=8
    )

    def column_of(kind):
        return jnp.broadcast_to(
            jnp.sum(
                jnp.where(here, tile[kind : kind + 1], 0.0), axis=1, keepdims=True
            ),
            (tokens, LANES),
        )

    exp_others, goal = column_of(0), column_of(1)
    exp_total = exp_others + jnp.exp(goal)
    loss_all[...] = jnp.log(exp_total) - goal
    goal_squash = goal * (1.0 / CAP)
    totals[0] = 1.0 / exp_total
    totals[1] = rounded(-exp_others / exp_total * (1.0 - goal_squash * goal_squash))

    def own_total(kind):
        return totals[kind, pl.ds(side * count_half + rep * own_half + sec // 2, 1), :]

    for b in range(batches):
        for w in range(width):
            k = b * width + w
            at = (k % 2) * count_half + rep * own_half + k // 2
            loss_ref[b : b + 1, w : w + 1] = loss_all[pl.ds(at, 1), 0:1]
    score_grad = ((powers / wide(exp_total) - jnp.where(mask, 1.0, 0.0)) * slope).astype(BF16)
    left_ref[pl.ds(0, tokens), :] = score_grad
    save_left = pltpu.make_async_copy(left_ref, left_hbm, recv_sem.at[OUT])
    save_left.start()
    head_rows = pl.ds(0, tokens)
    save_head = pltpu.make_async_copy(
        right_ref.at[head_rows], right_hbm.at[head_rows], recv_sem.at[OUT + 1]
    )
    save_head.start()

    def backward():
        take(grad_in, recv_sem.at[GRAD])
        take(goal_in, recv_sem.at[GOAL])
        goal_row = total(goal_in)
        grad = total(grad_in) * own_total(0) + goal_row * own_total(1)
        grad = spread_rows(grad) * gain_wide[layers]

        def back(normed, scale, grad):
            mean = jnp.sum(grad * normed, axis=1, keepdims=True) * (1.0 / dim)
            return scale * (grad - normed * mean)

        dy = rounded(back(*norm(layer_in[layers]), grad))

        def layer(step, dy):
            index = layers - 1 - step
            gain, first, second = weights(index)
            scale = kept[index, 0][:, 0:1]
            normed = layer_in[index] * scale
            hidden_grad = jnp.sum(dy * second, axis=1, keepdims=True)
            pre_grad = rounded(hidden_grad * kept[index, 1][:, 0:1])
            act_grad = jnp.sum(pre_grad * first, axis=0, keepdims=True)
            return rounded(dy + back(normed, scale, act_grad * gain))

        pack_row(lax.fori_loop(0, layers, layer, dy, unroll=2), emb_out)

    if_own(backward)
    gather(EMB, emb_out, emb_in)

    def store_emb(lanes, part):
        right_ref[pl.ds(tokens, tokens), lanes] = part.astype(BF16)

    unpack(emb_in, store_emb)
    emb_rows = pl.ds(tokens, tokens)
    save_emb = pltpu.make_async_copy(
        right_ref.at[emb_rows], right_hbm.at[emb_rows], recv_sem.at[OUT + 2]
    )
    save_emb.start()

    take(idbuf.at[pl.ds(0, replicas - 1)], send_sem.at[IDS])
    for phase, _, buf in stores:
        if half > 1:
            take(buf.at[0, pl.ds(0, half - 1)], send_sem.at[phase])
        take(buf.at[0], send_sem.at[phase + RELAY])
    take(stat_in.at[pl.ds(0, devices - 1)], send_sem.at[STAT])

    def owned():
        take(look_pair.at[pl.ds(0, count_half - 1)], send_sem.at[LOOK])
        take(goal_pair.at[pl.ds(0, count_half - 1)], send_sem.at[GOAL])
        take(grad_pair.at[pl.ds(0, count_half - 1)], send_sem.at[GRAD])
        take(look_in.at[pl.ds(0, devices // 2 - 1)], send_sem.at[HEAD])
        take(grad_in.at[pl.ds(0, devices // 2 - 1)], send_sem.at[EMB])

    if_own(owned)
    if not all_own:

        @pl.when(jnp.logical_not(own))
        def _():
            take(look_pair, send_sem.at[LOOK])
            take(goal_pair, send_sem.at[GOAL])
            take(grad_pair, send_sem.at[GRAD])
    save_left.wait()
    save_head.wait()
    save_emb.wait()


def table_kernel(loss_in, left_hbm, right_hbm, loss_out, out_hbm, left, right, out, sem, out_sem):
    tokens = left.shape[0] // 3
    steps, _, step = out.shape
    moves = [pltpu.make_async_copy(left_hbm, left, sem.at[2 * steps])]
    moves[0].start()
    for i in range(steps):
        lanes = pl.ds(i * step, step)
        for part in range(2):
            count = 2 * tokens if part == 0 else tokens
            moves.append(
                pltpu.make_async_copy(
                    right_hbm.at[pl.ds(part * tokens, count), lanes],
                    right.at[i, pl.ds(2 * part * tokens, count)],
                    sem.at[2 * i + part],
                )
            )
            moves[-1].start()
    loss_out[...] = loss_in[...]
    moves[0].wait()
    across = left[...].astype(F32).T.astype(BF16)
    saves = []
    for i in range(steps):
        moves[2 * i + 1].wait()
        moves[2 * i + 2].wait()
        out[i] = jnp.dot(across, right[i], preferred_element_type=F32).astype(BF16)
        saves.append(
            pltpu.make_async_copy(
                out.at[i], out_hbm.at[:, pl.ds(i * step, step)], out_sem.at[i]
            )
        )
        saves[-1].start()
    for save in saves:
        save.wait()


def per_device(token_ids, target_ids, table, norm_gain, w_in, w_out, final_gain):
    sections, replicas = lax.axis_size("section"), lax.axis_size("dp")
    batches, width = token_ids.shape
    rows_dev, dim = table.shape
    rank = w_in.shape[2]
    per_dp = batches * width
    tokens = replicas * per_dp
    devices = sections * replicas
    chunks = dim // LANES
    pad = (chunks + 7) // 8 * 8
    assert per_dp <= sections and tokens % 8 == 0
    assert chunks % 2 == 0 and rows_dev % LANES == 0
    assert per_dp % 2 == 0 and sections % 2 == 0
    assert tokens <= LANES
    block = (pad // 8, 8, LANES)
    vmem = pl.BlockSpec(memory_space=pltpu.VMEM)
    hbm = pl.BlockSpec(memory_space=pltpu.HBM)
    token_loss, left, right = pl.pallas_call(
        functools.partial(cascade, sections, replicas, per_dp, pad),
        out_shape=(
            jax.ShapeDtypeStruct((batches, width), F32),
            jax.ShapeDtypeStruct((3 * tokens, rows_dev), BF16),
            jax.ShapeDtypeStruct((2 * tokens, dim), BF16),
        ),
        in_specs=[vmem, vmem, hbm, vmem, vmem, hbm, hbm],
        out_specs=(vmem, hbm, hbm),
        scratch_shapes=[
            pltpu.VMEM((3 * tokens, rows_dev), BF16),
            pltpu.VMEM((2 * tokens, dim), BF16),
            pltpu.VMEM((tokens, LANES), F32),
            pltpu.VMEM((2 * per_dp, LANES), jnp.int32),
            pltpu.VMEM((replicas, 2 * per_dp, LANES), jnp.int32),
            pltpu.VMEM((2, tokens, LANES), jnp.int32),
            pltpu.VMEM((2, sections // 2, 2, dim), BF16),
            pltpu.VMEM((2, sections // 2, 2, 1, rank, dim), BF16),
            pltpu.VMEM((2, sections // 2, 2, 1, rank, dim), BF16),
            pltpu.VMEM((tokens * pad, LANES), F32),
            pltpu.VMEM((2, tokens // 2) + block, BF16),
            pltpu.VMEM((devices // 2,) + block, BF16),
            pltpu.VMEM((pad, LANES), F32),
            pltpu.VMEM((2 * sections + 1, 8, dim), F32),
            pltpu.VMEM(block, BF16),
            pltpu.VMEM((2, tokens // 2) + block, BF16),
            pltpu.VMEM((2, LANES), F32),
            pltpu.VMEM((devices, 2, LANES), F32),
            pltpu.VMEM((2, tokens // 2) + block, BF16),
            pltpu.VMEM((devices // 2,) + block, BF16),
            pltpu.VMEM(block, BF16),
            pltpu.VMEM((2, tokens // 2) + block, BF16),
            pltpu.VMEM((rows_dev, dim), BF16),
            pltpu.VMEM((2 * sections + 1, 8, dim), F32),
            pltpu.VMEM((2 * sections, 2, 8, LANES), F32),
            pltpu.VMEM((tokens // 2,) + block, BF16),
            pltpu.VMEM((tokens // 2,) + block, BF16),
            pltpu.VMEM((2, tokens // 2) + block, BF16),
            pltpu.VMEM((tokens // 2,) + block, BF16),
            pltpu.VMEM((devices // 2,) + block, BF16),
            pltpu.VMEM((2, tokens, LANES), F32),
            pltpu.SemaphoreType.DMA((40,)),
            pltpu.SemaphoreType.DMA((40,)),
        ],
        compiler_params=pltpu.CompilerParams(
            collective_id=0, has_side_effects=True, vmem_limit_bytes=63400000
        ),
        name="cascade",
    )(token_ids, target_ids, table, norm_gain[:, 0], final_gain, w_in, w_out)
    steps = 6
    step = dim // steps
    return pl.pallas_call(
        table_kernel,
        out_shape=(
            jax.ShapeDtypeStruct((batches, width), F32),
            jax.ShapeDtypeStruct((rows_dev, dim), BF16),
        ),
        in_specs=[vmem, hbm, hbm],
        out_specs=(vmem, hbm),
        scratch_shapes=[
            pltpu.VMEM((3 * tokens, rows_dev), BF16),
            pltpu.VMEM((steps, 3 * tokens, step), BF16),
            pltpu.VMEM((steps, rows_dev, step), BF16),
            pltpu.SemaphoreType.DMA((2 * steps + 1,)),
            pltpu.SemaphoreType.DMA((steps,)),
        ],
        name="table_grad",
    )(token_loss, left, right)


def solution(mesh):
    return jax.shard_map(
        per_device,
        mesh=mesh,
        in_specs=(
            P(None, "dp"),
            P(None, "dp"),
            P(("section", "dp"), None),
            P(None, "section", None),
            P(None, "section", None, None),
            P(None, "section", None, None),
            P(),
        ),
        out_specs=(P(None, "dp"), P(("section", "dp"), None)),
        check_vma=False,
    )
```

```python
import functools
import math

import jax
import jax.numpy as jnp
import ml_dtypes
import numpy as np
from jax import lax
from jax.experimental import pallas as pl
from jax.experimental.pallas import tpu as pltpu
from jax.sharding import PartitionSpec as P

EPS = 1e-06
CAP = 30.0
GELU_C = 0.7978845608028654
LANES = 128
F32 = jnp.float32
BF16 = jnp.bfloat16
IDS, LOOK, HEAD, STAT, GRAD, EMB = range(6)
ACROSS, MATE, RELAY = 6, 8, 10
TABLE = 12
PAIR = 13
GOAL = 20
OUT = 34


def gelu_tanh(values):
    return 0.5 * values * (1.0 + jnp.tanh(GELU_C * (values + 0.044715 * values * values * values)))


def gelu_slope(values):
    inner = jnp.tanh(GELU_C * (values + 0.044715 * values * values * values))
    return 0.5 * (1.0 + inner) + 0.5 * values * (1.0 - inner * inner) * GELU_C * (
        1.0 + 3.0 * 0.044715 * values * values
    )


def rounded(values):
    return values.astype(BF16).astype(F32)


def cascade(
    sections, replicas, per_dp, pad,
    rank, token_ref, target_ref, table_hbm, gain_ref, fgain_ref, win_ref, wout_ref,
    loss_ref, left_hbm, right_hbm,
    left_ref, right_ref, loss_all, ids_ref, idbuf, idrow, packed, gain_wide, first_wide, second_wide, flat, look_out, look_in, tok, layer_in,
    head_out, head_in, stat_out, stat_in, grad_out, grad_in, emb_out, emb_in,
    table_ref, kept, look_pair, grad_pair, goal_out, goal_pair, goal_in, totals, send_sem, recv_sem,
):
    devices = sections * replicas
    tokens = replicas * per_dp
    rows_dev, dim = table_ref.shape
    chunks = dim // LANES
    head_ref = right_ref.at[pl.ds(0, tokens)]
    layers = 2 * sections
    scale_in = math.sqrt(dim)
    sec, rep = lax.axis_index("section"), lax.axis_index("dp")
    me = sec * replicas + rep
    offset = me * rows_dev
    all_own = per_dp == sections
    own = sec < per_dp
    own_half = per_dp // 2
    count_half = tokens // 2
    half = sections // 2
    side, partner = sec % 2, sec + 1 - 2 * (sec % 2)
    my_half = rep * own_half + sec // 2
    if not all_own:
        my_half = jnp.where(own, my_half, -1)

    def if_own(body):
        if all_own:
            body()
        else:
            pl.when(own)(body)

    def spread(phase, count, first, target, skip, src, dst):
        def step(i, _):
            at = lax.rem(first + i, count)

            @pl.when(at != skip)
            def _():
                pltpu.make_async_remote_copy(
                    src_ref=src(at),
                    dst_ref=dst,
                    send_sem=send_sem.at[phase],
                    recv_sem=recv_sem.at[phase],
                    device_id=target(at),
                    device_id_type=pl.DeviceIdType.MESH,
                ).start()

            @pl.when(at == skip)
            def _():
                pltpu.make_async_copy(src(at), dst, recv_sem.at[phase]).start()

            return 0

        lax.fori_loop(0, count, step, 0, unroll=8)

    def take(ref, sem):
        pltpu.make_async_copy(ref, ref, sem).wait()

    def any_device(n):
        return (n // replicas, n % replicas)

    def token_device(h):
        return (2 * (h % own_half) + side, h // own_half)

    def side_device(q):
        return (2 * (q // replicas) + side, q % replicas)

    side_me = (sec // 2) * replicas + rep

    def pair_copy(phase, src, dst):
        return pltpu.make_async_remote_copy(
            src_ref=src,
            dst_ref=dst,
            send_sem=send_sem.at[phase],
            recv_sem=recv_sem.at[phase],
            device_id=(partner, rep),
            device_id_type=pl.DeviceIdType.MESH,
        )

    load = pltpu.make_async_copy(table_hbm, table_ref, recv_sem.at[TABLE])
    load.start()
    barrier = pltpu.get_barrier_semaphore()

    def greet(i, _):
        n = lax.rem(me + 1 + i, devices)
        pl.semaphore_signal(
            barrier, inc=1, device_id=any_device(n), device_id_type=pl.DeviceIdType.MESH
        )
        return 0

    lax.fori_loop(0, devices - 1, greet, 0, unroll=8)
    flat[...] = jnp.zeros_like(flat)
    tok[...] = jnp.zeros_like(tok)
    row = lax.broadcasted_iota(jnp.int32, (2 * per_dp, LANES), 0)
    made = jnp.zeros((2 * per_dp, LANES), jnp.int32)
    batches, width = token_ref.shape
    for b in range(batches):
        for w in range(width):
            k = b * width + w
            made = jnp.where(row == k, token_ref[b : b + 1, w : w + 1], made)
            made = jnp.where(row == per_dp + k, target_ref[b : b + 1, w : w + 1], made)
    ids_ref[...] = made
    group = sec // 2
    blocks = (pad // 8, 8, LANES)

    def pack_row(values):
        for j in range(chunks):
            tok[j : j + 1, :] = values[:, j * LANES : (j + 1) * LANES]
        return tok[...]

    both_gains = gain_ref[...].astype(F32)
    for c in range(2):
        for slot, src in ((0, win_ref), (rank, wout_ref)):
            values = src[c, 0].astype(F32)
            for j in range(chunks):
                flat[pl.ds(j, rank, stride=pad), :] = values[:, j * LANES : (j + 1) * LANES]
            packed[c, side, group, pl.ds(slot, rank)] = (
                flat[pl.ds(0, rank * pad), :].reshape((rank,) + blocks).astype(BF16)
            )
        packed[c, side, group, 2 * rank] = (
            pack_row(both_gains[c : c + 1]).reshape(blocks).astype(BF16)
        )
    final_gain = pack_row(fgain_ref[...].astype(F32).reshape(1, dim))
    pl.semaphore_wait(barrier, devices - 1)

    spread(IDS, replicas, rep, lambda d: (sec, d), rep, lambda d: ids_ref, idbuf.at[rep])
    def send_weights(phase, c, block, target):
        pltpu.make_async_remote_copy(
            src_ref=packed.at[c, side, block],
            dst_ref=packed.at[c, side, block],
            send_sem=send_sem.at[phase + c],
            recv_sem=recv_sem.at[phase + c],
            device_id=target,
            device_id_type=pl.DeviceIdType.MESH,
        ).start()

    def across(c):
        for i in range(1, half):
            send_weights(ACROSS, c, group, (2 * lax.rem(group + i, half) + side, rep))

    def relay_weights(c):
        if half > 1:
            take(packed.at[c, 0, pl.ds(0, half - 1)], recv_sem.at[ACROSS + c])
        for i in range(1, half):
            send_weights(RELAY, c, lax.rem(group + i, half), (partner, rep))

    def widen_weights(c):
        take(packed.at[c, 0, 0], recv_sem.at[MATE + c])
        if half > 1:
            take(packed.at[c, 0, pl.ds(0, half - 1)], recv_sem.at[RELAY + c])

        def widen(s, _):
            at = (c, s % 2, s // 2)
            gain = packed[at + (2 * rank,)].astype(F32)
            first = packed[at + (pl.ds(0, rank),)].astype(F32)
            gain_wide[c * sections + s] = gain.reshape(pad, LANES)
            second = packed[at + (pl.ds(rank, rank),)].astype(F32)
            first_wide[c * sections + s] = first.reshape(rank, pad, LANES)
            second_wide[c * sections + s] = second.reshape(rank, pad, LANES)
            return 0

        lax.fori_loop(0, sections, widen, 0)

    across(0)
    for c in range(2):
        send_weights(MATE, c, group, (partner, rep))

    take(idbuf, recv_sem.at[IDS])
    across(1)
    for d in range(replicas):
        for kind in range(2):
            for k in range(per_dp):
                at = (k % 2) * count_half + d * own_half + k // 2
                idrow[kind, pl.ds(at, 1), :] = idbuf[
                    d, pl.ds(kind * per_dp + k, 1), :
                ]
    wide = lambda value: jnp.concatenate([value] * (rows_dev // LANES), axis=1)
    column = lax.broadcasted_iota(jnp.int32, (tokens, rows_dev), 1) + offset
    chosen = jnp.where(wide(idrow[0]) == column, 1.0, 0.0).astype(BF16)
    mask = wide(idrow[1]) == column
    high_scale = float(np.float32(scale_in).astype(ml_dtypes.bfloat16))
    low_scale = float(np.float32(scale_in - high_scale).astype(ml_dtypes.bfloat16))
    left_ref[pl.ds(tokens, tokens), :] = (chosen.astype(F32) * high_scale).astype(BF16)
    left_ref[pl.ds(2 * tokens, tokens), :] = (chosen.astype(F32) * low_scale).astype(BF16)
    load.wait()

    def scatter(left, phase, out, pair, into):
        for j in range(0, chunks, 2):
            part = jnp.dot(
                left, table_ref[:, j * LANES : (j + 2) * LANES], preferred_element_type=F32
            )
            flat[pl.ds(j, tokens, stride=pad), :] = part[:, :LANES]
            flat[pl.ds(j + 1, tokens, stride=pad), :] = part[:, LANES:]
        mine = pl.ds(pl.multiple_of(side * (count_half * pad), 8), count_half * pad)
        away = pl.ds(pl.multiple_of((1 - side) * (count_half * pad), 8), count_half * pad)
        blocks = (count_half, pad // 8, 8, LANES)
        out[1 - side] = flat[away, :].reshape(blocks).astype(BF16)
        swap = pair_copy(phase + PAIR, out.at[1 - side], pair)
        swap.start()
        swap.wait()
        out[side] = (flat[mine, :].reshape(blocks) + pair[...].astype(F32)).astype(BF16)
        spread(
            phase, count_half, rep * own_half + sec // 2, token_device, my_half,
            lambda h: out.at[side, h], into.at[side_me],
        )

    def total(into):
        return lax.fori_loop(
            0, devices // 2, lambda n, acc: acc + into[n].astype(F32),
            jnp.zeros((pad // 8, 8, LANES), F32),
            unroll=4,
        ).reshape(pad, LANES)

    def whole(values):
        return jnp.sum(jnp.sum(values, axis=0, keepdims=True), axis=1, keepdims=True)

    def dots(values, rows):
        part = jnp.sum((values[None] * rows).reshape((rank,) + blocks), axis=1)
        return jnp.sum(jnp.sum(part, axis=1), axis=1, keepdims=True)

    def combine(weights, rows):
        wide_weights = jnp.broadcast_to(weights, (rank, LANES))
        acc = wide_weights[0:1] * rows[0]
        for k in range(1, rank):
            acc = acc + wide_weights[k : k + 1] * rows[k]
        return acc

    def norm_scale(x):
        return lax.rsqrt(whole(x * x) * (1.0 / dim) + EPS)

    def gather(phase, block, into):
        if_own(
            lambda: spread(
                phase, devices // 2, side_me, side_device, side_me,
                lambda n: block, into.at[side, my_half],
            )
        )
        take(into.at[side], recv_sem.at[phase])
        relay = pair_copy(phase + PAIR, into.at[side], into.at[side])
        relay.start()
        relay.wait()

    def unpack(into, out):
        flat[...] = into[...].astype(F32).reshape(tokens * pad, LANES)
        for j in range(chunks):
            out(slice(j * LANES, (j + 1) * LANES), flat[pl.ds(j, tokens, stride=pad), :])

    scatter(chosen, LOOK, look_out, look_pair, look_in)
    relay_weights(0)
    scatter(jnp.where(mask, 1.0, 0.0).astype(BF16), GOAL, goal_out, goal_pair, goal_in)
    relay_weights(1)
    widen_weights(0)
    widen_weights(1)

    def forward():
        take(look_in, recv_sem.at[LOOK])
        x = rounded(total(look_in) * scale_in)

        def layer(index, x):
            layer_in[index] = x
            scale = norm_scale(x)
            pre = dots(rounded(x * scale * gain_wide[index]), first_wide[index])
            hidden = rounded(gelu_tanh(pre))
            kept[index, 0] = jnp.broadcast_to(scale, (rank, LANES))
            kept[index, 1] = jnp.broadcast_to(gelu_slope(pre), (rank, LANES))
            kept[index, 2] = jnp.broadcast_to(pre, (rank, LANES))
            return rounded(x + combine(hidden, second_wide[index]))

        x = lax.fori_loop(0, layers, layer, x, unroll=2)
        layer_in[layers] = x
        head_out[...] = (x * norm_scale(x) * final_gain).reshape(blocks).astype(BF16)

    if_own(forward)
    gather(HEAD, head_out, head_in)

    def store_head(lanes, part):
        right_ref[pl.ds(0, tokens), lanes] = part.astype(BF16)

    unpack(head_in, store_head)

    scores = lax.dot_general(
        head_ref[...], table_ref[...], (((1,), (1,)), ((), ())), preferred_element_type=F32
    )
    squash = jnp.tanh(scores / CAP)
    capped = CAP * squash
    powers = jnp.exp(capped)
    slope = 1.0 - squash * squash
    others = jnp.where(mask, 0.0, powers)
    exp_sum = jnp.sum(others, axis=1, keepdims=True)
    goal = jnp.sum(jnp.where(mask, capped, 0.0), axis=1, keepdims=True)
    lane = lax.broadcasted_iota(jnp.int32, (tokens, LANES), 1)
    here = lane == lax.broadcasted_iota(jnp.int32, (tokens, LANES), 0)
    stat_out[0:1, :] = jnp.sum(jnp.where(here, exp_sum, 0.0), axis=0, keepdims=True)
    stat_out[1:2, :] = jnp.sum(jnp.where(here, goal, 0.0), axis=0, keepdims=True)
    spread(STAT, devices, me, any_device, me, lambda n: stat_out, stat_in.at[me])
    scatter((others * slope).astype(BF16), GRAD, grad_out, grad_pair, grad_in)
    take(stat_in, recv_sem.at[STAT])
    tile = lax.fori_loop(
        0, devices, lambda n, acc: acc + stat_in[n], jnp.zeros((2, LANES), F32), unroll=8
    )

    def column_of(kind):
        return jnp.broadcast_to(
            jnp.sum(
                jnp.where(here, tile[kind : kind + 1], 0.0), axis=1, keepdims=True
            ),
            (tokens, LANES),
        )

    exp_others, goal = column_of(0), column_of(1)
    exp_total = exp_others + jnp.exp(goal)
    loss_all[...] = jnp.log(exp_total) - goal
    goal_squash = goal * (1.0 / CAP)
    totals[0] = 1.0 / exp_total
    totals[1] = rounded(-exp_others / exp_total * (1.0 - goal_squash * goal_squash))

    def own_total(kind):
        return totals[kind, pl.ds(side * count_half + rep * own_half + sec // 2, 1), :]

    for b in range(batches):
        for w in range(width):
            k = b * width + w
            at = (k % 2) * count_half + rep * own_half + k // 2
            loss_ref[b : b + 1, w : w + 1] = loss_all[pl.ds(at, 1), 0:1]
    score_grad = ((powers / wide(exp_total) - jnp.where(mask, 1.0, 0.0)) * slope).astype(BF16)
    left_ref[pl.ds(0, tokens), :] = score_grad
    save_left = pltpu.make_async_copy(left_ref, left_hbm, recv_sem.at[OUT])
    save_left.start()
    head_rows = pl.ds(0, tokens)
    save_head = pltpu.make_async_copy(
        right_ref.at[head_rows], right_hbm.at[head_rows], recv_sem.at[OUT + 1]
    )
    save_head.start()

    def backward():
        take(grad_in, recv_sem.at[GRAD])
        take(goal_in, recv_sem.at[GOAL])
        goal_row = total(goal_in)
        grad = total(grad_in) * own_total(0) + goal_row * own_total(1)
        grad = grad * final_gain
        x = layer_in[layers]
        scale = norm_scale(x)
        normed = x * scale
        dy = rounded(scale * (grad - normed * (whole(grad * normed) * (1.0 / dim))))

        def layer(step, dy):
            index = layers - 1 - step
            scale = kept[index, 0][0:1, 0:1]
            pre_grad = rounded(dots(dy, second_wide[index]) * kept[index, 1][:, 0:1])
            mean = jnp.sum(pre_grad * kept[index, 2][:, 0:1], axis=0, keepdims=True)
            act_grad = combine(pre_grad, first_wide[index]) * gain_wide[index]
            back = act_grad - layer_in[index] * (scale * mean * (1.0 / dim))
            return rounded(dy + scale * back)

        dy = lax.fori_loop(0, layers, layer, dy, unroll=2)
        emb_out[...] = dy.reshape(blocks).astype(BF16)

    if_own(backward)
    gather(EMB, emb_out, emb_in)

    def store_emb(lanes, part):
        right_ref[pl.ds(tokens, tokens), lanes] = part.astype(BF16)

    unpack(emb_in, store_emb)
    emb_rows = pl.ds(tokens, tokens)
    save_emb = pltpu.make_async_copy(
        right_ref.at[emb_rows], right_hbm.at[emb_rows], recv_sem.at[OUT + 2]
    )
    save_emb.start()

    take(idbuf.at[pl.ds(0, replicas - 1)], send_sem.at[IDS])
    for c in range(2):
        take(packed.at[c, 0, 0], send_sem.at[MATE + c])
        if half > 1:
            take(packed.at[c, 0, pl.ds(0, half - 1)], send_sem.at[ACROSS + c])
            take(packed.at[c, 0, pl.ds(0, half - 1)], send_sem.at[RELAY + c])
    take(stat_in.at[pl.ds(0, devices - 1)], send_sem.at[STAT])

    def owned():
        take(look_pair.at[pl.ds(0, count_half - 1)], send_sem.at[LOOK])
        take(goal_pair.at[pl.ds(0, count_half - 1)], send_sem.at[GOAL])
        take(grad_pair.at[pl.ds(0, count_half - 1)], send_sem.at[GRAD])
        take(look_in.at[pl.ds(0, devices // 2 - 1)], send_sem.at[HEAD])
        take(grad_in.at[pl.ds(0, devices // 2 - 1)], send_sem.at[EMB])

    if_own(owned)
    if not all_own:

        @pl.when(jnp.logical_not(own))
        def _():
            take(look_pair, send_sem.at[LOOK])
            take(goal_pair, send_sem.at[GOAL])
            take(grad_pair, send_sem.at[GRAD])
    save_left.wait()
    save_head.wait()
    save_emb.wait()


def table_kernel(loss_in, left_hbm, right_hbm, loss_out, out_hbm, left, right, out, sem, out_sem):
    tokens = left.shape[0] // 3
    steps = 4
    rows = out.shape[0] // steps
    moves = [
        pltpu.make_async_copy(left_hbm, left, sem.at[0]),
        pltpu.make_async_copy(right_hbm, right.at[pl.ds(0, 2 * tokens)], sem.at[1]),
        pltpu.make_async_copy(
            right_hbm.at[pl.ds(tokens, tokens)], right.at[pl.ds(2 * tokens, tokens)], sem.at[2]
        ),
        pltpu.make_async_copy(loss_in, loss_out, sem.at[3]),
    ]
    for move in moves:
        move.start()
    moves[0].wait()
    across = left[...].astype(F32).T.astype(BF16)
    moves[1].wait()
    moves[2].wait()
    for i in range(steps):
        at = pl.ds(i * rows, rows)
        out[at, :] = jnp.dot(
            across[i * rows : (i + 1) * rows], right[...], preferred_element_type=F32
        ).astype(BF16)
        save = pltpu.make_async_copy(out.at[at], out_hbm.at[at], out_sem.at[i])
        save.start()
        moves.append(save)
    for move in moves[3:]:
        move.wait()


def per_device(token_ids, target_ids, table, norm_gain, w_in, w_out, final_gain):
    sections, replicas = lax.axis_size("section"), lax.axis_size("dp")
    batches, width = token_ids.shape
    rows_dev, dim = table.shape
    rank = w_in.shape[2]
    per_dp = batches * width
    tokens = replicas * per_dp
    devices = sections * replicas
    chunks = dim // LANES
    pad = (chunks + 7) // 8 * 8
    assert per_dp <= sections and tokens % 8 == 0
    assert chunks % 2 == 0 and rows_dev % LANES == 0
    assert per_dp % 2 == 0 and sections % 2 == 0
    assert tokens <= LANES
    block = (pad // 8, 8, LANES)
    vmem = pl.BlockSpec(memory_space=pltpu.VMEM)
    hbm = pl.BlockSpec(memory_space=pltpu.HBM)
    token_loss, left, right = pl.pallas_call(
        functools.partial(cascade, sections, replicas, per_dp, pad, rank),
        out_shape=(
            jax.ShapeDtypeStruct((batches, width), F32),
            jax.ShapeDtypeStruct((3 * tokens, rows_dev), BF16),
            jax.ShapeDtypeStruct((2 * tokens, dim), BF16),
        ),
        in_specs=[vmem, vmem, hbm, vmem, vmem, vmem, vmem],
        out_specs=(vmem, hbm, hbm),
        scratch_shapes=[
            pltpu.VMEM((3 * tokens, rows_dev), BF16),
            pltpu.VMEM((2 * tokens, dim), BF16),
            pltpu.VMEM((tokens, LANES), F32),
            pltpu.VMEM((2 * per_dp, LANES), jnp.int32),
            pltpu.VMEM((replicas, 2 * per_dp, LANES), jnp.int32),
            pltpu.VMEM((2, tokens, LANES), jnp.int32),
            pltpu.VMEM((2, 2, sections // 2, 2 * rank + 1) + block, BF16),
            pltpu.VMEM((2 * sections, pad, LANES), F32),
            pltpu.VMEM((2 * sections, rank, pad, LANES), F32),
            pltpu.VMEM((2 * sections, rank, pad, LANES), F32),
            pltpu.VMEM((tokens * pad, LANES), F32),
            pltpu.VMEM((2, tokens // 2) + block, BF16),
            pltpu.VMEM((devices // 2,) + block, BF16),
            pltpu.VMEM((pad, LANES), F32),
            pltpu.VMEM((2 * sections + 1, pad, LANES), F32),
            pltpu.VMEM(block, BF16),
            pltpu.VMEM((2, tokens // 2) + block, BF16),
            pltpu.VMEM((2, LANES), F32),
            pltpu.VMEM((devices, 2, LANES), F32),
            pltpu.VMEM((2, tokens // 2) + block, BF16),
            pltpu.VMEM((devices // 2,) + block, BF16),
            pltpu.VMEM(block, BF16),
            pltpu.VMEM((2, tokens // 2) + block, BF16),
            pltpu.VMEM((rows_dev, dim), BF16),
            pltpu.VMEM((2 * sections, 3, rank, LANES), F32),
            pltpu.VMEM((tokens // 2,) + block, BF16),
            pltpu.VMEM((tokens // 2,) + block, BF16),
            pltpu.VMEM((2, tokens // 2) + block, BF16),
            pltpu.VMEM((tokens // 2,) + block, BF16),
            pltpu.VMEM((devices // 2,) + block, BF16),
            pltpu.VMEM((2, tokens, LANES), F32),
            pltpu.SemaphoreType.DMA((40,)),
            pltpu.SemaphoreType.DMA((40,)),
        ],
        compiler_params=pltpu.CompilerParams(
            collective_id=0, has_side_effects=True, vmem_limit_bytes=63400000
        ),
        name="cascade",
    )(token_ids, target_ids, table, norm_gain[:, 0], final_gain, w_in, w_out)
    return pl.pallas_call(
        table_kernel,
        out_shape=(
            jax.ShapeDtypeStruct((batches, width), F32),
            jax.ShapeDtypeStruct((rows_dev, dim), BF16),
        ),
        in_specs=[hbm] * 3,
        out_specs=(hbm, hbm),
        scratch_shapes=[
            pltpu.VMEM((3 * tokens, rows_dev), BF16),
            pltpu.VMEM((3 * tokens, dim), BF16),
            pltpu.VMEM((rows_dev, dim), BF16),
            pltpu.SemaphoreType.DMA((4,)),
            pltpu.SemaphoreType.DMA((4,)),
        ],
        name="table_grad",
    )(token_loss, left, right)


def solution(mesh):
    return jax.shard_map(
        per_device,
        mesh=mesh,
        in_specs=(
            P(None, "dp"),
            P(None, "dp"),
            P(("section", "dp"), None),
            P(None, "section", None),
            P(None, "section", None, None),
            P(None, "section", None, None),
            P(),
        ),
        out_specs=(P(None, "dp"), P(("section", "dp"), None)),
        check_vma=False,
    )
```

```python
import functools
import math

import jax
import jax.numpy as jnp
import ml_dtypes
import numpy as np
from jax import lax
from jax.experimental import pallas as pl
from jax.experimental.pallas import tpu as pltpu
from jax.sharding import PartitionSpec as P

EPS = 1e-06
CAP = 30.0
GELU_C = 0.7978845608028654
LANES = 128
F32 = jnp.float32
BF16 = jnp.bfloat16
IDS, LOOK, HEAD, STAT, GRAD, EMB = range(6)
ACROSS, MATE, RELAY = 6, 8, 10
TABLE, GOAL, TABLE_MATE, HEAD_MATE, EMB_MATE, STAT_MATE, SCORE_MATE = range(12, 19)
OUT, IN, SEMS = 19, 25, 31


def gelu_tanh(values):
    return 0.5 * values * (1.0 + jnp.tanh(GELU_C * (values + 0.044715 * values * values * values)))


def gelu_slope(values):
    inner = jnp.tanh(GELU_C * (values + 0.044715 * values * values * values))
    return 0.5 * (1.0 + inner) + 0.5 * values * (1.0 - inner * inner) * GELU_C * (
        1.0 + 3.0 * 0.044715 * values * values
    )


def rounded(values):
    return values.astype(BF16).astype(F32)


def cascade(
    sections, replicas, per_dp, pad,
    rank, token_hbm, target_hbm, table_hbm, gain_hbm, fgain_hbm, win_hbm, wout_hbm,
    loss_hbm, left_hbm, right_hbm,
    token_ref, target_ref, gain_ref, fgain_ref, win_ref, wout_ref, loss_ref,
    left_ref, right_ref, ids_ref, idbuf, idrow, packed, gain_wide, first_wide, second_wide,
    flat, tok, look_out, look_in, goal_out, goal_in, layer_in, kept, head_out, head_in,
    stat_out, stat_in, stat_sum, totals, score_out, score_in, grad_out, grad_in,
    emb_out, emb_in, table_ref, send_sem, recv_sem,
):
    devices = sections * replicas
    tokens = replicas * per_dp
    rows_dev = table_ref.shape[0] // 2
    dim = table_ref.shape[1]
    chunks = dim // LANES
    layers = 2 * sections
    scale_in = math.sqrt(dim)
    sec, rep = lax.axis_index("section"), lax.axis_index("dp")
    me = sec * replicas + rep
    all_own = per_dp == sections
    own = sec < per_dp
    own_half = per_dp // 2
    count_half = tokens // 2
    half = sections // 2
    group, side = sec // 2, sec % 2
    partner = sec + 1 - 2 * side
    side_me = group * replicas + rep
    my_half = rep * own_half + group
    if not all_own:
        my_half = jnp.where(own, my_half, -1)
    blocks = (pad // 8, 8, LANES)
    my_rows = pl.ds(pl.multiple_of(side * count_half, 16), count_half)
    mate_rows = pl.ds(pl.multiple_of((1 - side) * count_half, 16), count_half)

    def if_own(body):
        if all_own:
            body()
        else:
            pl.when(own)(body)

    def spread(phase, count, first, target, skip, src, dst):
        def step(i, _):
            at = lax.rem(first + i, count)

            @pl.when(at != skip)
            def _():
                pltpu.make_async_remote_copy(
                    src_ref=src(at),
                    dst_ref=dst,
                    send_sem=send_sem.at[phase],
                    recv_sem=recv_sem.at[phase],
                    device_id=target(at),
                    device_id_type=pl.DeviceIdType.MESH,
                ).start()

            @pl.when(at == skip)
            def _():
                pltpu.make_async_copy(src(at), dst, recv_sem.at[phase]).start()

            return 0

        lax.fori_loop(0, count, step, 0, unroll=8)

    def take(ref, sem):
        pltpu.make_async_copy(ref, ref, sem).wait()

    def token_device(h):
        return (2 * (h % own_half) + side, h // own_half)

    def side_device(q):
        return (2 * (q // replicas) + side, q % replicas)

    def pair_copy(phase, src, dst):
        return pltpu.make_async_remote_copy(
            src_ref=src,
            dst_ref=dst,
            send_sem=send_sem.at[phase],
            recv_sem=recv_sem.at[phase],
            device_id=(partner, rep),
            device_id_type=pl.DeviceIdType.MESH,
        )

    barrier = pltpu.get_barrier_semaphore()

    def signal(target):
        pl.semaphore_signal(
            barrier, inc=1, device_id=target, device_id_type=pl.DeviceIdType.MESH
        )

    def greet(i, _):
        signal(side_device(lax.rem(side_me + 1 + i, devices // 2)))
        return 0

    lax.fori_loop(0, devices // 2 - 1, greet, 0, unroll=8)
    signal((partner, rep))
    inputs = [
        pltpu.make_async_copy(src, dst, recv_sem.at[IN + i])
        for i, (src, dst) in enumerate(
            (
                (token_hbm, token_ref),
                (target_hbm, target_ref),
                (win_hbm, win_ref),
                (wout_hbm, wout_ref),
                (gain_hbm, gain_ref),
                (fgain_hbm, fgain_ref),
            )
        )
    ]
    for move in inputs:
        move.start()
    own_table = table_ref.at[pl.ds(0, rows_dev)]
    load = pltpu.make_async_copy(table_hbm, own_table, recv_sem.at[TABLE])
    load.start()
    flat[...] = jnp.zeros_like(flat)
    tok[...] = jnp.zeros_like(tok)
    inputs[0].wait()
    inputs[1].wait()
    row = lax.broadcasted_iota(jnp.int32, (2 * per_dp, LANES), 0)
    made = jnp.zeros((2 * per_dp, LANES), jnp.int32)
    batches, width = token_ref.shape
    for b in range(batches):
        for w in range(width):
            k = b * width + w
            made = jnp.where(row == k, token_ref[b : b + 1, w : w + 1], made)
            made = jnp.where(row == per_dp + k, target_ref[b : b + 1, w : w + 1], made)
    ids_ref[...] = made
    for move in inputs[2:]:
        move.wait()

    def pack_row(values):
        for j in range(chunks):
            tok[j : j + 1, :] = values[:, j * LANES : (j + 1) * LANES]
        return tok[...]

    both_gains = gain_ref[...].astype(F32)
    for c in range(2):
        for slot, src in ((0, win_ref), (rank, wout_ref)):
            values = src[c, 0].astype(F32)
            for j in range(chunks):
                flat[pl.ds(j, rank, stride=pad), :] = values[:, j * LANES : (j + 1) * LANES]
            packed[c, side, group, pl.ds(slot, rank)] = (
                flat[pl.ds(0, rank * pad), :].reshape((rank,) + blocks).astype(BF16)
            )
        packed[c, side, group, 2 * rank] = (
            pack_row(both_gains[c : c + 1]).reshape(blocks).astype(BF16)
        )
    final_gain = pack_row(fgain_ref[...].astype(F32).reshape(1, dim))
    pl.semaphore_wait(barrier, devices // 2)

    spread(IDS, replicas, rep, lambda d: (sec, d), rep, lambda d: ids_ref, idbuf.at[rep])
    table_mate = pair_copy(TABLE_MATE, table_hbm, table_ref.at[pl.ds(rows_dev, rows_dev)])
    table_mate.start()

    def send_weights(phase, c, block, target):
        pltpu.make_async_remote_copy(
            src_ref=packed.at[c, side, block],
            dst_ref=packed.at[c, side, block],
            send_sem=send_sem.at[phase + c],
            recv_sem=recv_sem.at[phase + c],
            device_id=target,
            device_id_type=pl.DeviceIdType.MESH,
        ).start()

    def across(c):
        for i in range(1, half):
            send_weights(ACROSS, c, group, (2 * lax.rem(group + i, half) + side, rep))

    def relay_weights(c):
        if half > 1:
            take(packed.at[c, 0, pl.ds(0, half - 1)], recv_sem.at[ACROSS + c])
        for i in range(1, half):
            send_weights(RELAY, c, lax.rem(group + i, half), (partner, rep))

    def widen_weights(c):
        take(packed.at[c, 0, 0], recv_sem.at[MATE + c])
        if half > 1:
            take(packed.at[c, 0, pl.ds(0, half - 1)], recv_sem.at[RELAY + c])

        def widen(s, _):
            at = (c, s % 2, s // 2)
            gain = packed[at + (2 * rank,)].astype(F32)
            first = packed[at + (pl.ds(0, rank),)].astype(F32)
            gain_wide[c * sections + s] = gain.reshape(pad, LANES)
            second = packed[at + (pl.ds(rank, rank),)].astype(F32)
            first_wide[c * sections + s] = first.reshape(rank, pad, LANES)
            second_wide[c * sections + s] = second.reshape(rank, pad, LANES)
            return 0

        lax.fori_loop(0, sections, widen, 0)

    across(0)
    for c in range(2):
        send_weights(MATE, c, group, (partner, rep))

    take(idbuf, recv_sem.at[IDS])
    across(1)
    for d in range(replicas):
        for kind in range(2):
            for k in range(per_dp):
                at = (k % 2) * count_half + d * own_half + k // 2
                idrow[kind, pl.ds(at, 1), :] = idbuf[
                    d, pl.ds(kind * per_dp + k, 1), :
                ]
    wide = lambda value: jnp.concatenate([value] * (rows_dev // LANES), axis=1)
    both = lambda value: jnp.concatenate([wide(value)] * 2, axis=1)
    place = lax.broadcasted_iota(jnp.int32, (tokens, rows_dev), 1) + me * rows_dev
    chosen = jnp.where(wide(idrow[0]) == place, 1.0, 0.0)
    high_scale = float(np.float32(scale_in).astype(ml_dtypes.bfloat16))
    low_scale = float(np.float32(scale_in - high_scale).astype(ml_dtypes.bfloat16))
    left_ref[pl.ds(tokens, tokens), :] = (chosen * high_scale).astype(BF16)
    left_ref[pl.ds(2 * tokens, tokens), :] = (chosen * low_scale).astype(BF16)
    column = lax.broadcasted_iota(jnp.int32, (count_half, 2 * rows_dev), 1)
    column = column + jnp.where(
        column < rows_dev, me * rows_dev, (partner * replicas + rep - 1) * rows_dev
    )
    picked = both(idrow[0, my_rows, :]) == column
    mask = both(idrow[1, my_rows, :]) == column
    load.wait()
    table_mate.wait_recv()

    def project(left, out):
        for j in range(0, chunks, 2):
            part = jnp.dot(
                left, table_ref[:, j * LANES : (j + 2) * LANES], preferred_element_type=F32
            )
            flat[pl.ds(j, count_half, stride=pad), :] = part[:, :LANES]
            flat[pl.ds(j + 1, count_half, stride=pad), :] = part[:, LANES:]
        rows = flat[pl.ds(0, count_half * pad), :]
        out[...] = rows.reshape((count_half,) + blocks).astype(BF16)

    def send_rows(phase, out, into):
        spread(
            phase, count_half, rep * own_half + group, token_device, my_half,
            lambda h: out.at[h], into.at[side_me],
        )

    def total(into):
        return lax.fori_loop(
            0, devices // 2, lambda n, acc: acc + into[n].astype(F32),
            jnp.zeros(blocks, F32),
            unroll=4,
        ).reshape(pad, LANES)

    def whole(values):
        return jnp.sum(jnp.sum(values, axis=0, keepdims=True), axis=1, keepdims=True)

    def dots(values, rows):
        part = jnp.sum((values[None] * rows).reshape((rank,) + blocks), axis=1)
        return jnp.sum(jnp.sum(part, axis=1), axis=1, keepdims=True)

    def combine(weights, rows):
        wide_weights = jnp.broadcast_to(weights, (rank, LANES))
        acc = wide_weights[0:1] * rows[0]
        for k in range(1, rank):
            acc = acc + wide_weights[k : k + 1] * rows[k]
        return acc

    def norm_scale(x):
        return lax.rsqrt(whole(x * x) * (1.0 / dim) + EPS)

    def gather(phase, block, into):
        if_own(
            lambda: spread(
                phase, devices // 2, side_me, side_device, side_me,
                lambda n: block, into.at[side, my_half],
            )
        )
        take(into.at[side], recv_sem.at[phase])

    def unpack(block, first, rows):
        flat[pl.ds(0, count_half * pad), :] = (
            block[...].astype(F32).reshape(count_half * pad, LANES)
        )
        for j in range(chunks):
            right_ref[first, rows, j * LANES : (j + 1) * LANES] = flat[
                pl.ds(j, count_half, stride=pad), :
            ].astype(BF16)

    project(jnp.where(picked, 1.0, 0.0).astype(BF16), look_out)
    send_rows(LOOK, look_out, look_in)
    relay_weights(0)
    project(jnp.where(mask, 1.0, 0.0).astype(BF16), goal_out)
    relay_weights(1)
    widen_weights(0)
    widen_weights(1)

    def forward():
        take(look_in, recv_sem.at[LOOK])
        x = rounded(total(look_in) * scale_in)

        def layer(index, x):
            layer_in[index] = x
            scale = norm_scale(x)
            pre = dots(rounded(x * scale * gain_wide[index]), first_wide[index])
            hidden = rounded(gelu_tanh(pre))
            kept[index, 0] = jnp.broadcast_to(scale, (rank, LANES))
            kept[index, 1] = jnp.broadcast_to(gelu_slope(pre), (rank, LANES))
            kept[index, 2] = jnp.broadcast_to(pre, (rank, LANES))
            return rounded(x + combine(hidden, second_wide[index]))

        x = lax.fori_loop(0, layers, layer, x, unroll=2)
        layer_in[layers] = x
        head_out[...] = (x * norm_scale(x) * final_gain).reshape(blocks).astype(BF16)

    if_own(forward)
    gather(HEAD, head_out, head_in)
    head_mate = pair_copy(HEAD_MATE, head_in.at[side], head_in.at[side])
    head_mate.start()
    send_rows(GOAL, goal_out, goal_in)
    unpack(head_in.at[side], 0, my_rows)
    scores = lax.dot_general(
        right_ref[0, my_rows, :], table_ref[...], (((1,), (1,)), ((), ())),
        preferred_element_type=F32,
    )
    squash = jnp.tanh(scores / CAP)
    capped = CAP * squash
    powers = jnp.exp(capped)
    slope = 1.0 - squash * squash
    others = jnp.where(mask, 0.0, powers)
    exp_sum = jnp.sum(others, axis=1, keepdims=True)
    goal = jnp.sum(jnp.where(mask, capped, 0.0), axis=1, keepdims=True)
    lane = lax.broadcasted_iota(jnp.int32, (count_half, LANES), 1)
    here = lane == lax.broadcasted_iota(jnp.int32, (count_half, LANES), 0)
    stat_out[0:1, :] = jnp.sum(jnp.where(here, exp_sum, 0.0), axis=0, keepdims=True)
    stat_out[1:2, :] = jnp.sum(jnp.where(here, goal, 0.0), axis=0, keepdims=True)
    spread(
        STAT, devices // 2, side_me, side_device, side_me, lambda n: stat_out, stat_in.at[side_me]
    )
    project((others * slope).astype(BF16), grad_out)
    send_rows(GRAD, grad_out, grad_in)

    take(stat_in, recv_sem.at[STAT])
    tile = lax.fori_loop(
        0, devices // 2, lambda n, acc: acc + stat_in[n], jnp.zeros((2, LANES), F32), unroll=8
    )
    stat_sum[side] = tile
    stat_mate = pair_copy(STAT_MATE, stat_sum.at[side], stat_sum.at[side])
    stat_mate.start()

    def column_of(kind):
        return jnp.broadcast_to(
            jnp.sum(jnp.where(here, tile[kind : kind + 1], 0.0), axis=1, keepdims=True),
            (count_half, LANES),
        )

    exp_others, goal = column_of(0), column_of(1)
    exp_total = exp_others + jnp.exp(goal)
    goal_squash = goal * (1.0 / CAP)
    totals[0] = 1.0 / exp_total
    totals[1] = rounded(-exp_others / exp_total * (1.0 - goal_squash * goal_squash))

    def own_total(kind):
        return totals[kind, pl.ds(jnp.maximum(my_half, 0), 1), :]

    score_grad = ((powers / both(exp_total) - jnp.where(mask, 1.0, 0.0)) * slope).astype(BF16)
    left_ref[my_rows, :] = score_grad[:, :rows_dev]
    score_out[...] = score_grad[:, rows_dev:]
    score_mate = pair_copy(SCORE_MATE, score_out, score_in)
    score_mate.start()
    head_mate.wait_recv()
    unpack(head_in.at[1 - side], 0, mate_rows)
    stat_mate.wait_recv()
    one = lax.broadcasted_iota(jnp.int32, (1, LANES), 1)
    for b in range(batches):
        for w in range(width):
            k = b * width + w
            sums = stat_sum[k % 2]
            losses = jnp.log(sums[0:1] + jnp.exp(sums[1:2])) - sums[1:2]
            loss_ref[b : b + 1, w : w + 1] = jnp.sum(
                jnp.where(one == rep * own_half + k // 2, losses, 0.0), axis=1, keepdims=True
            )
    score_mate.wait_recv()
    left_ref[mate_rows, :] = score_in[...]
    saves = [
        pltpu.make_async_copy(left_ref, left_hbm, recv_sem.at[OUT]),
        pltpu.make_async_copy(right_ref.at[0], right_hbm.at[0], recv_sem.at[OUT + 1]),
        pltpu.make_async_copy(loss_ref, loss_hbm, recv_sem.at[OUT + 2]),
    ]
    for save in saves:
        save.start()

    def backward():
        take(grad_in, recv_sem.at[GRAD])
        take(goal_in, recv_sem.at[GOAL])
        goal_row = total(goal_in)
        grad = total(grad_in) * own_total(0) + goal_row * own_total(1)
        grad = grad * final_gain
        x = layer_in[layers]
        scale = norm_scale(x)
        normed = x * scale
        dy = rounded(scale * (grad - normed * (whole(grad * normed) * (1.0 / dim))))

        def layer(step, dy):
            index = layers - 1 - step
            scale = kept[index, 0][0:1, 0:1]
            pre_grad = rounded(dots(dy, second_wide[index]) * kept[index, 1][:, 0:1])
            mean = jnp.sum(pre_grad * kept[index, 2][:, 0:1], axis=0, keepdims=True)
            act_grad = combine(pre_grad, first_wide[index]) * gain_wide[index]
            back = act_grad - layer_in[index] * (scale * mean * (1.0 / dim))
            return rounded(dy + scale * back)

        dy = lax.fori_loop(0, layers, layer, dy, unroll=2)
        emb_out[...] = dy.reshape(blocks).astype(BF16)

    if_own(backward)
    gather(EMB, emb_out, emb_in)
    emb_mate = pair_copy(EMB_MATE, emb_in.at[side], emb_in.at[side])
    emb_mate.start()

    def finish(block, rows, sem):
        unpack(block, 1, rows)
        save = pltpu.make_async_copy(right_ref.at[1, rows], right_hbm.at[1, rows], sem)
        save.start()
        saves.append(save)

    finish(emb_in.at[side], my_rows, recv_sem.at[OUT + 3])
    emb_mate.wait_recv()
    finish(emb_in.at[1 - side], mate_rows, recv_sem.at[OUT + 4])

    for move in (table_mate, head_mate, stat_mate, score_mate, emb_mate):
        move.wait_send()
    take(idbuf.at[pl.ds(0, replicas - 1)], send_sem.at[IDS])
    for c in range(2):
        take(packed.at[c, 0, 0], send_sem.at[MATE + c])
        if half > 1:
            take(packed.at[c, 0, pl.ds(0, half - 1)], send_sem.at[ACROSS + c])
            take(packed.at[c, 0, pl.ds(0, half - 1)], send_sem.at[RELAY + c])
    take(stat_in.at[pl.ds(0, devices // 2 - 1)], send_sem.at[STAT])
    sent = ((LOOK, look_out), (GOAL, goal_out), (GRAD, grad_out))

    def owned():
        for phase, out in sent:
            take(out.at[pl.ds(0, count_half - 1)], send_sem.at[phase])
        take(look_in.at[pl.ds(0, devices // 2 - 1)], send_sem.at[HEAD])
        take(grad_in.at[pl.ds(0, devices // 2 - 1)], send_sem.at[EMB])

    if_own(owned)
    if not all_own:

        @pl.when(jnp.logical_not(own))
        def _():
            for phase, out in sent:
                take(out, send_sem.at[phase])

    for save in saves:
        save.wait()


def table_kernel(loss_in, left_hbm, right_hbm, loss_out, out_hbm, left, right, out, sem, out_sem):
    tokens = left.shape[0] // 3
    steps = 4
    rows = out.shape[0] // steps
    moves = [
        pltpu.make_async_copy(left_hbm, left, sem.at[0]),
        pltpu.make_async_copy(right_hbm.at[0], right.at[pl.ds(0, tokens)], sem.at[1]),
        pltpu.make_async_copy(right_hbm.at[1], right.at[pl.ds(tokens, tokens)], sem.at[2]),
        pltpu.make_async_copy(right_hbm.at[1], right.at[pl.ds(2 * tokens, tokens)], sem.at[3]),
        pltpu.make_async_copy(loss_in, loss_out, sem.at[4]),
    ]
    for move in moves:
        move.start()
    moves[0].wait()
    across = left[...].astype(F32).T.astype(BF16)
    for move in moves[1:4]:
        move.wait()
    for i in range(steps):
        at = pl.ds(i * rows, rows)
        out[at, :] = jnp.dot(
            across[i * rows : (i + 1) * rows], right[...], preferred_element_type=F32
        ).astype(BF16)
        save = pltpu.make_async_copy(out.at[at], out_hbm.at[at], out_sem.at[i])
        save.start()
        moves.append(save)
    for move in moves[4:]:
        move.wait()


def per_device(token_ids, target_ids, table, norm_gain, w_in, w_out, final_gain):
    sections, replicas = lax.axis_size("section"), lax.axis_size("dp")
    batches, width = token_ids.shape
    rows_dev, dim = table.shape
    rank = w_in.shape[2]
    per_dp = batches * width
    tokens = replicas * per_dp
    devices = sections * replicas
    chunks = dim // LANES
    pad = (chunks + 7) // 8 * 8
    assert per_dp <= sections and tokens % 32 == 0
    assert chunks % 2 == 0 and rows_dev % LANES == 0
    assert per_dp % 2 == 0 and sections % 2 == 0
    assert tokens <= LANES
    block = (pad // 8, 8, LANES)
    vmem = pl.BlockSpec(memory_space=pltpu.VMEM)
    hbm = pl.BlockSpec(memory_space=pltpu.HBM)
    token_loss, left, right = pl.pallas_call(
        functools.partial(cascade, sections, replicas, per_dp, pad, rank),
        out_shape=(
            jax.ShapeDtypeStruct((batches, width), F32),
            jax.ShapeDtypeStruct((3 * tokens, rows_dev), BF16),
            jax.ShapeDtypeStruct((2, tokens, dim), BF16),
        ),
        in_specs=[hbm] * 7,
        out_specs=(hbm,) * 3,
        scratch_shapes=[
            pltpu.VMEM((batches, width), jnp.int32),
            pltpu.VMEM((batches, width), jnp.int32),
            pltpu.VMEM((2, dim), BF16),
            pltpu.VMEM((dim,), BF16),
            pltpu.VMEM((2, 1, rank, dim), BF16),
            pltpu.VMEM((2, 1, rank, dim), BF16),
            pltpu.VMEM((batches, width), F32),
            pltpu.VMEM((3 * tokens, rows_dev), BF16),
            pltpu.VMEM((2, tokens, dim), BF16),
            pltpu.VMEM((2 * per_dp, LANES), jnp.int32),
            pltpu.VMEM((replicas, 2 * per_dp, LANES), jnp.int32),
            pltpu.VMEM((2, tokens, LANES), jnp.int32),
            pltpu.VMEM((2, 2, sections // 2, 2 * rank + 1) + block, BF16),
            pltpu.VMEM((2 * sections, pad, LANES), F32),
            pltpu.VMEM((2 * sections, rank, pad, LANES), F32),
            pltpu.VMEM((2 * sections, rank, pad, LANES), F32),
            pltpu.VMEM((max(tokens // 2, rank) * pad, LANES), F32),
            pltpu.VMEM((pad, LANES), F32),
            pltpu.VMEM((tokens // 2,) + block, BF16),
            pltpu.VMEM((devices // 2,) + block, BF16),
            pltpu.VMEM((tokens // 2,) + block, BF16),
            pltpu.VMEM((devices // 2,) + block, BF16),
            pltpu.VMEM((2 * sections + 1, pad, LANES), F32),
            pltpu.VMEM((2 * sections, 3, rank, LANES), F32),
            pltpu.VMEM(block, BF16),
            pltpu.VMEM((2, tokens // 2) + block, BF16),
            pltpu.VMEM((2, LANES), F32),
            pltpu.VMEM((devices // 2, 2, LANES), F32),
            pltpu.VMEM((2, 2, LANES), F32),
            pltpu.VMEM((2, tokens // 2, LANES), F32),
            pltpu.VMEM((tokens // 2, rows_dev), BF16),
            pltpu.VMEM((tokens // 2, rows_dev), BF16),
            pltpu.VMEM((tokens // 2,) + block, BF16),
            pltpu.VMEM((devices // 2,) + block, BF16),
            pltpu.VMEM(block, BF16),
            pltpu.VMEM((2, tokens // 2) + block, BF16),
            pltpu.VMEM((2 * rows_dev, dim), BF16),
            pltpu.SemaphoreType.DMA((SEMS,)),
            pltpu.SemaphoreType.DMA((SEMS,)),
        ],
        compiler_params=pltpu.CompilerParams(
            collective_id=0, has_side_effects=True, vmem_limit_bytes=63400000
        ),
        name="cascade",
    )(token_ids, target_ids, table, norm_gain[:, 0], final_gain, w_in, w_out)
    return pl.pallas_call(
        table_kernel,
        out_shape=(
            jax.ShapeDtypeStruct((batches, width), F32),
            jax.ShapeDtypeStruct((rows_dev, dim), BF16),
        ),
        in_specs=[hbm] * 3,
        out_specs=(hbm, hbm),
        scratch_shapes=[
            pltpu.VMEM((3 * tokens, rows_dev), BF16),
            pltpu.VMEM((3 * tokens, dim), BF16),
            pltpu.VMEM((rows_dev, dim), BF16),
            pltpu.SemaphoreType.DMA((5,)),
            pltpu.SemaphoreType.DMA((4,)),
        ],
        name="table_grad",
    )(token_loss, left, right)


def solution(mesh):
    return jax.shard_map(
        per_device,
        mesh=mesh,
        in_specs=(
            P(None, "dp"),
            P(None, "dp"),
            P(("section", "dp"), None),
            P(None, "section", None),
            P(None, "section", None, None),
            P(None, "section", None, None),
            P(),
        ),
        out_specs=(P(None, "dp"), P(("section", "dp"), None)),
        check_vma=False,
    )
```

```python
import functools
import math

import jax
import jax.numpy as jnp
import ml_dtypes
import numpy as np
from jax import lax
from jax.experimental import pallas as pl
from jax.experimental.pallas import tpu as pltpu
from jax.sharding import PartitionSpec as P

EPS = 1e-06
CAP = 30.0
GELU_C = 0.7978845608028654
LANES = 128
F32 = jnp.float32
BF16 = jnp.bfloat16
IDS, LOOK, HEAD, STAT, GRAD, EMB = range(6)
ACROSS, MATE, RELAY = 6, 8, 10
TABLE, GOAL, TABLE_MATE, HEAD_MATE, EMB_MATE, STAT_MATE, SCORE_MATE = range(12, 19)
OUT, IN, SEMS = 19, 25, 31


def gelu_tanh(values):
    return 0.5 * values * (1.0 + jnp.tanh(GELU_C * (values + 0.044715 * values * values * values)))


def gelu_slope(values):
    inner = jnp.tanh(GELU_C * (values + 0.044715 * values * values * values))
    return 0.5 * (1.0 + inner) + 0.5 * values * (1.0 - inner * inner) * GELU_C * (
        1.0 + 3.0 * 0.044715 * values * values
    )


def rounded(values):
    return values.astype(BF16).astype(F32)


def cascade(
    sections, replicas, per_dp, pad,
    rank, token_hbm, target_hbm, table_hbm, gain_hbm, fgain_hbm, win_hbm, wout_hbm,
    loss_hbm, left_ref, right_ref,
    token_ref, target_ref, gain_ref, fgain_ref, win_ref, wout_ref, loss_ref,
    ids_ref, idbuf, idrow, packed, gain_wide, first_wide, second_wide,
    flat, tok, look_out, look_in, goal_out, goal_in, layer_in, kept, head_out, head_in,
    stat_out, stat_in, stat_sum, totals, score_out, score_in, grad_out, grad_in,
    emb_out, emb_in, table_ref, send_sem, recv_sem,
):
    devices = sections * replicas
    tokens = replicas * per_dp
    rows_dev = table_ref.shape[0] // 2
    dim = table_ref.shape[1]
    chunks = dim // LANES
    layers = 2 * sections
    scale_in = math.sqrt(dim)
    sec, rep = lax.axis_index("section"), lax.axis_index("dp")
    me = sec * replicas + rep
    all_own = per_dp == sections
    own = sec < per_dp
    own_half = per_dp // 2
    count_half = tokens // 2
    half = sections // 2
    group, side = sec // 2, sec % 2
    partner = sec + 1 - 2 * side
    side_me = group * replicas + rep
    my_half = rep * own_half + group
    if not all_own:
        my_half = jnp.where(own, my_half, -1)
    blocks = (pad // 8, 8, LANES)
    my_rows = pl.ds(pl.multiple_of(side * count_half, 16), count_half)
    mate_rows = pl.ds(pl.multiple_of((1 - side) * count_half, 16), count_half)

    def if_own(body):
        if all_own:
            body()
        else:
            pl.when(own)(body)

    def spread(phase, count, first, target, skip, src, dst, part=0, parts=1):
        def step(i, _):
            at = lax.rem(first + parts * i + part, count)

            @pl.when(at != skip)
            def _():
                pltpu.make_async_remote_copy(
                    src_ref=src(at),
                    dst_ref=dst,
                    send_sem=send_sem.at[phase],
                    recv_sem=recv_sem.at[phase],
                    device_id=target(at),
                    device_id_type=pl.DeviceIdType.MESH,
                ).start()

            @pl.when(at == skip)
            def _():
                pltpu.make_async_copy(src(at), dst, recv_sem.at[phase]).start()

            return 0

        lax.fori_loop(0, count // parts, step, 0, unroll=8)

    def take(ref, sem):
        pltpu.make_async_copy(ref, ref, sem).wait()

    def token_device(h):
        return (2 * (h % own_half) + side, h // own_half)

    def side_device(q):
        return (2 * (q // replicas) + side, q % replicas)

    def pair_copy(phase, src, dst):
        return pltpu.make_async_remote_copy(
            src_ref=src,
            dst_ref=dst,
            send_sem=send_sem.at[phase],
            recv_sem=recv_sem.at[phase],
            device_id=(partner, rep),
            device_id_type=pl.DeviceIdType.MESH,
        )

    barrier = pltpu.get_barrier_semaphore()

    def signal(target):
        pl.semaphore_signal(
            barrier, inc=1, device_id=target, device_id_type=pl.DeviceIdType.MESH
        )

    def greet(i, _):
        signal(side_device(lax.rem(side_me + 1 + i, devices // 2)))
        return 0

    lax.fori_loop(0, devices // 2 - 1, greet, 0, unroll=8)
    signal((partner, rep))
    inputs = [
        pltpu.make_async_copy(src, dst, recv_sem.at[IN + i])
        for i, (src, dst) in enumerate(
            (
                (token_hbm, token_ref),
                (target_hbm, target_ref),
                (win_hbm, win_ref),
                (wout_hbm, wout_ref),
                (gain_hbm, gain_ref),
                (fgain_hbm, fgain_ref),
            )
        )
    ]
    for move in inputs:
        move.start()
    own_table = table_ref.at[pl.ds(0, rows_dev)]
    load = pltpu.make_async_copy(table_hbm, own_table, recv_sem.at[TABLE])
    load.start()
    flat[...] = jnp.zeros_like(flat)
    tok[...] = jnp.zeros_like(tok)
    inputs[0].wait()
    inputs[1].wait()
    row = lax.broadcasted_iota(jnp.int32, (2 * per_dp, LANES), 0)
    made = jnp.zeros((2 * per_dp, LANES), jnp.int32)
    batches, width = token_ref.shape
    for b in range(batches):
        for w in range(width):
            k = b * width + w
            made = jnp.where(row == k, token_ref[b : b + 1, w : w + 1], made)
            made = jnp.where(row == per_dp + k, target_ref[b : b + 1, w : w + 1], made)
    ids_ref[...] = made
    for move in inputs[2:]:
        move.wait()

    def pack_row(values):
        for j in range(chunks):
            tok[j : j + 1, :] = values[:, j * LANES : (j + 1) * LANES]
        return tok[...]

    both_gains = gain_ref[...].astype(F32)
    for c in range(2):
        for slot, src in ((0, win_ref), (rank, wout_ref)):
            values = src[c, 0].astype(F32)
            for j in range(chunks):
                flat[pl.ds(j, rank, stride=pad), :] = values[:, j * LANES : (j + 1) * LANES]
            packed[c, side, group, pl.ds(slot, rank)] = (
                flat[pl.ds(0, rank * pad), :].reshape((rank,) + blocks).astype(BF16)
            )
        packed[c, side, group, 2 * rank] = (
            pack_row(both_gains[c : c + 1]).reshape(blocks).astype(BF16)
        )
    final_gain = pack_row(fgain_ref[...].astype(F32).reshape(1, dim))
    pl.semaphore_wait(barrier, devices // 2)

    spread(IDS, replicas, rep, lambda d: (sec, d), rep, lambda d: ids_ref, idbuf.at[rep])
    table_mate = pair_copy(TABLE_MATE, table_hbm, table_ref.at[pl.ds(rows_dev, rows_dev)])
    table_mate.start()

    def send_weights(phase, c, block, target):
        pltpu.make_async_remote_copy(
            src_ref=packed.at[c, side, block],
            dst_ref=packed.at[c, side, block],
            send_sem=send_sem.at[phase + c],
            recv_sem=recv_sem.at[phase + c],
            device_id=target,
            device_id_type=pl.DeviceIdType.MESH,
        ).start()

    def across(c):
        for i in range(1, half):
            send_weights(ACROSS, c, group, (2 * lax.rem(group + i, half) + side, rep))

    def relay_weights(c):
        if half > 1:
            take(packed.at[c, 0, pl.ds(0, half - 1)], recv_sem.at[ACROSS + c])
        for i in range(1, half):
            send_weights(RELAY, c, lax.rem(group + i, half), (partner, rep))

    def widen_weights(c):
        take(packed.at[c, 0, 0], recv_sem.at[MATE + c])
        if half > 1:
            take(packed.at[c, 0, pl.ds(0, half - 1)], recv_sem.at[RELAY + c])

        def widen(s, _):
            at = (c, s % 2, s // 2)
            gain = packed[at + (2 * rank,)].astype(F32)
            first = packed[at + (pl.ds(0, rank),)].astype(F32)
            gain_wide[c * sections + s] = gain.reshape(pad, LANES)
            second = packed[at + (pl.ds(rank, rank),)].astype(F32)
            first_wide[c * sections + s] = first.reshape(rank, pad, LANES)
            second_wide[c * sections + s] = second.reshape(rank, pad, LANES)
            return 0

        lax.fori_loop(0, sections, widen, 0)

    across(0)
    for c in range(2):
        send_weights(MATE, c, group, (partner, rep))

    take(idbuf, recv_sem.at[IDS])
    across(1)
    for d in range(replicas):
        for kind in range(2):
            for k in range(per_dp):
                at = (k % 2) * count_half + d * own_half + k // 2
                idrow[kind, pl.ds(at, 1), :] = idbuf[
                    d, pl.ds(kind * per_dp + k, 1), :
                ]
    wide = lambda value: jnp.concatenate([value] * (rows_dev // LANES), axis=1)
    both = lambda value: jnp.concatenate([wide(value)] * 2, axis=1)
    place = lax.broadcasted_iota(jnp.int32, (tokens, rows_dev), 1) + me * rows_dev
    chosen = jnp.where(wide(idrow[0]) == place, 1.0, 0.0)
    high_scale = float(np.float32(scale_in).astype(ml_dtypes.bfloat16))
    low_scale = float(np.float32(scale_in - high_scale).astype(ml_dtypes.bfloat16))
    left_ref[pl.ds(tokens, tokens), :] = (chosen * high_scale).astype(BF16)
    left_ref[pl.ds(2 * tokens, tokens), :] = (chosen * low_scale).astype(BF16)
    column = lax.broadcasted_iota(jnp.int32, (count_half, 2 * rows_dev), 1)
    column = column + jnp.where(
        column < rows_dev, me * rows_dev, (partner * replicas + rep - 1) * rows_dev
    )
    picked = both(idrow[0, my_rows, :]) == column
    mask = both(idrow[1, my_rows, :]) == column
    load.wait()
    table_mate.wait_recv()

    def project(left, out):
        for j in range(0, chunks, 2):
            part = jnp.dot(
                left, table_ref[:, j * LANES : (j + 2) * LANES], preferred_element_type=F32
            )
            flat[pl.ds(j, count_half, stride=pad), :] = part[:, :LANES]
            flat[pl.ds(j + 1, count_half, stride=pad), :] = part[:, LANES:]
        rows = flat[pl.ds(0, count_half * pad), :]
        out[...] = rows.reshape((count_half,) + blocks).astype(BF16)

    def send_rows(phase, out, into, part=0, parts=1):
        spread(
            phase, count_half, rep * own_half + group, token_device, my_half,
            lambda h: out.at[h], into.at[side_me], part, parts,
        )

    def total(into):
        return lax.fori_loop(
            0, devices // 2, lambda n, acc: acc + into[n].astype(F32),
            jnp.zeros(blocks, F32),
            unroll=4,
        ).reshape(pad, LANES)

    def whole(values):
        return jnp.sum(jnp.sum(values, axis=0, keepdims=True), axis=1, keepdims=True)

    def dots(values, rows):
        part = jnp.sum((values[None] * rows).reshape((rank,) + blocks), axis=1)
        return jnp.sum(jnp.sum(part, axis=1), axis=1, keepdims=True)

    def combine(weights, rows):
        wide_weights = jnp.broadcast_to(weights, (rank, LANES))
        acc = wide_weights[0:1] * rows[0]
        for k in range(1, rank):
            acc = acc + wide_weights[k : k + 1] * rows[k]
        return acc

    def norm_scale(x):
        return lax.rsqrt(whole(x * x) * (1.0 / dim) + EPS)

    def gather(phase, block, into):
        if_own(
            lambda: spread(
                phase, devices // 2, side_me, side_device, side_me,
                lambda n: block, into.at[side, my_half],
            )
        )
        take(into.at[side], recv_sem.at[phase])

    def unpack(block, first, rows):
        flat[pl.ds(0, count_half * pad), :] = (
            block[...].astype(F32).reshape(count_half * pad, LANES)
        )
        for j in range(chunks):
            right_ref[first, rows, j * LANES : (j + 1) * LANES] = flat[
                pl.ds(j, count_half, stride=pad), :
            ].astype(BF16)

    project(jnp.where(picked, 1.0, 0.0).astype(BF16), look_out)
    send_rows(LOOK, look_out, look_in)
    relay_weights(0)
    project(jnp.where(mask, 1.0, 0.0).astype(BF16), goal_out)
    relay_weights(1)
    widen_weights(0)
    widen_weights(1)

    if_own(lambda: take(look_in, recv_sem.at[LOOK]))
    send_rows(GOAL, goal_out, goal_in, 0, 2)

    def forward():
        x = rounded(total(look_in) * scale_in)

        def layer(index, x):
            layer_in[index] = x
            scale = norm_scale(x)
            pre = dots(rounded(x * scale * gain_wide[index]), first_wide[index])
            hidden = rounded(gelu_tanh(pre))
            kept[index, 0] = jnp.broadcast_to(scale, (rank, LANES))
            kept[index, 1] = jnp.broadcast_to(gelu_slope(pre), (rank, LANES))
            kept[index, 2] = jnp.broadcast_to(pre, (rank, LANES))
            return rounded(x + combine(hidden, second_wide[index]))

        x = lax.fori_loop(0, layers, layer, x, unroll=2)
        layer_in[layers] = x
        head_out[...] = (x * norm_scale(x) * final_gain).reshape(blocks).astype(BF16)

    if_own(forward)
    gather(HEAD, head_out, head_in)
    head_mate = pair_copy(HEAD_MATE, head_in.at[side], head_in.at[side])
    head_mate.start()
    send_rows(GOAL, goal_out, goal_in, 1, 2)
    unpack(head_in.at[side], 0, my_rows)
    scores = lax.dot_general(
        right_ref[0, my_rows, :], table_ref[...], (((1,), (1,)), ((), ())),
        preferred_element_type=F32,
    )
    squash = jnp.tanh(scores / CAP)
    capped = CAP * squash
    powers = jnp.exp(capped)
    slope = 1.0 - squash * squash
    others = jnp.where(mask, 0.0, powers)
    exp_sum = jnp.sum(others, axis=1, keepdims=True)
    goal = jnp.sum(jnp.where(mask, capped, 0.0), axis=1, keepdims=True)
    lane = lax.broadcasted_iota(jnp.int32, (count_half, LANES), 1)
    here = lane == lax.broadcasted_iota(jnp.int32, (count_half, LANES), 0)
    stat_out[0:1, :] = jnp.sum(jnp.where(here, exp_sum, 0.0), axis=0, keepdims=True)
    stat_out[1:2, :] = jnp.sum(jnp.where(here, goal, 0.0), axis=0, keepdims=True)
    spread(
        STAT, devices // 2, side_me, side_device, side_me, lambda n: stat_out, stat_in.at[side_me]
    )
    project((others * slope).astype(BF16), grad_out)
    send_rows(GRAD, grad_out, grad_in)

    take(stat_in, recv_sem.at[STAT])
    tile = lax.fori_loop(
        0, devices // 2, lambda n, acc: acc + stat_in[n], jnp.zeros((2, LANES), F32), unroll=8
    )
    stat_sum[side] = tile
    stat_mate = pair_copy(STAT_MATE, stat_sum.at[side], stat_sum.at[side])
    stat_mate.start()

    def column_of(kind):
        return jnp.broadcast_to(
            jnp.sum(jnp.where(here, tile[kind : kind + 1], 0.0), axis=1, keepdims=True),
            (count_half, LANES),
        )

    exp_others, goal = column_of(0), column_of(1)
    exp_total = exp_others + jnp.exp(goal)
    goal_squash = goal * (1.0 / CAP)
    totals[0] = 1.0 / exp_total
    totals[1] = rounded(-exp_others / exp_total * (1.0 - goal_squash * goal_squash))

    def own_total(kind):
        return totals[kind, pl.ds(jnp.maximum(my_half, 0), 1), :]

    score_grad = ((powers / both(exp_total) - jnp.where(mask, 1.0, 0.0)) * slope).astype(BF16)
    left_ref[my_rows, :] = score_grad[:, :rows_dev]
    score_out[...] = score_grad[:, rows_dev:]
    score_mate = pair_copy(SCORE_MATE, score_out, score_in)
    score_mate.start()
    head_mate.wait_recv()
    unpack(head_in.at[1 - side], 0, mate_rows)
    stat_mate.wait_recv()
    one = lax.broadcasted_iota(jnp.int32, (1, LANES), 1)
    for b in range(batches):
        for w in range(width):
            k = b * width + w
            sums = stat_sum[k % 2]
            losses = jnp.log(sums[0:1] + jnp.exp(sums[1:2])) - sums[1:2]
            loss_ref[b : b + 1, w : w + 1] = jnp.sum(
                jnp.where(one == rep * own_half + k // 2, losses, 0.0), axis=1, keepdims=True
            )
    score_mate.wait_recv()
    left_ref[mate_rows, :] = score_in[...]
    saves = [
        pltpu.make_async_copy(loss_ref, loss_hbm, recv_sem.at[OUT + 2]),
    ]
    for save in saves:
        save.start()

    def backward():
        take(grad_in, recv_sem.at[GRAD])
        take(goal_in, recv_sem.at[GOAL])
        goal_row = total(goal_in)
        grad = total(grad_in) * own_total(0) + goal_row * own_total(1)
        grad = grad * final_gain
        x = layer_in[layers]
        scale = norm_scale(x)
        normed = x * scale
        dy = rounded(scale * (grad - normed * (whole(grad * normed) * (1.0 / dim))))

        def layer(step, dy):
            index = layers - 1 - step
            scale = kept[index, 0][0:1, 0:1]
            pre_grad = rounded(dots(dy, second_wide[index]) * kept[index, 1][:, 0:1])
            mean = jnp.sum(pre_grad * kept[index, 2][:, 0:1], axis=0, keepdims=True)
            act_grad = combine(pre_grad, first_wide[index]) * gain_wide[index]
            back = act_grad - layer_in[index] * (scale * mean * (1.0 / dim))
            return rounded(dy + scale * back)

        dy = lax.fori_loop(0, layers, layer, dy, unroll=2)
        emb_out[...] = dy.reshape(blocks).astype(BF16)

    if_own(backward)
    gather(EMB, emb_out, emb_in)
    emb_mate = pair_copy(EMB_MATE, emb_in.at[side], emb_in.at[side])
    emb_mate.start()

    unpack(emb_in.at[side], 1, my_rows)
    emb_mate.wait_recv()
    unpack(emb_in.at[1 - side], 1, mate_rows)

    for move in (table_mate, head_mate, stat_mate, score_mate, emb_mate):
        move.wait_send()
    take(idbuf.at[pl.ds(0, replicas - 1)], send_sem.at[IDS])
    for c in range(2):
        take(packed.at[c, 0, 0], send_sem.at[MATE + c])
        if half > 1:
            take(packed.at[c, 0, pl.ds(0, half - 1)], send_sem.at[ACROSS + c])
            take(packed.at[c, 0, pl.ds(0, half - 1)], send_sem.at[RELAY + c])
    take(stat_in.at[pl.ds(0, devices // 2 - 1)], send_sem.at[STAT])
    sent = ((LOOK, look_out), (GOAL, goal_out), (GRAD, grad_out))

    def owned():
        for phase, out in sent:
            take(out.at[pl.ds(0, count_half - 1)], send_sem.at[phase])
        take(look_in.at[pl.ds(0, devices // 2 - 1)], send_sem.at[HEAD])
        take(grad_in.at[pl.ds(0, devices // 2 - 1)], send_sem.at[EMB])

    if_own(owned)
    if not all_own:

        @pl.when(jnp.logical_not(own))
        def _():
            for phase, out in sent:
                take(out, send_sem.at[phase])

    for save in saves:
        save.wait()


def table_kernel(loss_in, left_ref, right_ref, loss_out, out_hbm, right, out, sem, out_sem):
    tokens = right_ref.shape[1]
    steps = out_sem.shape[0]
    rows = out.shape[0] // steps
    moves = [pltpu.make_async_copy(loss_in, loss_out, sem)]
    moves[0].start()
    right[pl.ds(0, tokens), :] = right_ref[0]
    right[pl.ds(tokens, tokens), :] = right_ref[1]
    right[pl.ds(2 * tokens, tokens), :] = right_ref[1]
    across = left_ref[...].astype(F32).T.astype(BF16)
    for i in range(steps):
        at = pl.ds(i * rows, rows)
        out[at, :] = jnp.dot(
            across[i * rows : (i + 1) * rows], right[...], preferred_element_type=F32
        ).astype(BF16)
        save = pltpu.make_async_copy(out.at[at], out_hbm.at[at], out_sem.at[i])
        save.start()
        moves.append(save)
    for move in moves:
        move.wait()


def per_device(token_ids, target_ids, table, norm_gain, w_in, w_out, final_gain):
    sections, replicas = lax.axis_size("section"), lax.axis_size("dp")
    batches, width = token_ids.shape
    rows_dev, dim = table.shape
    rank = w_in.shape[2]
    per_dp = batches * width
    tokens = replicas * per_dp
    devices = sections * replicas
    chunks = dim // LANES
    pad = (chunks + 7) // 8 * 8
    assert per_dp <= sections and tokens % 32 == 0
    assert chunks % 2 == 0 and rows_dev % LANES == 0
    assert per_dp % 2 == 0 and sections % 2 == 0
    assert tokens <= LANES
    block = (pad // 8, 8, LANES)
    vmem = pl.BlockSpec(memory_space=pltpu.VMEM)
    hbm = pl.BlockSpec(memory_space=pltpu.HBM)
    inputs = (token_ids, target_ids, table, norm_gain[:, 0], final_gain, w_in, w_out)
    token_loss, left, right = pl.pallas_call(
        functools.partial(cascade, sections, replicas, per_dp, pad, rank),
        out_shape=(
            jax.ShapeDtypeStruct((batches, width), F32),
            pltpu.VMEM((3 * tokens, rows_dev), BF16),
            pltpu.VMEM((2, tokens, dim), BF16),
        ),
        in_specs=[hbm] * 7,
        out_specs=(hbm, vmem, vmem),
        scratch_shapes=[
            pltpu.VMEM((batches, width), jnp.int32),
            pltpu.VMEM((batches, width), jnp.int32),
            pltpu.VMEM((2, dim), BF16),
            pltpu.VMEM((dim,), BF16),
            pltpu.VMEM((2, 1, rank, dim), BF16),
            pltpu.VMEM((2, 1, rank, dim), BF16),
            pltpu.VMEM((batches, width), F32),
            pltpu.VMEM((2 * per_dp, LANES), jnp.int32),
            pltpu.VMEM((replicas, 2 * per_dp, LANES), jnp.int32),
            pltpu.VMEM((2, tokens, LANES), jnp.int32),
            pltpu.VMEM((2, 2, sections // 2, 2 * rank + 1) + block, BF16),
            pltpu.VMEM((2 * sections, pad, LANES), F32),
            pltpu.VMEM((2 * sections, rank, pad, LANES), F32),
            pltpu.VMEM((2 * sections, rank, pad, LANES), F32),
            pltpu.VMEM((max(tokens // 2, rank) * pad, LANES), F32),
            pltpu.VMEM((pad, LANES), F32),
            pltpu.VMEM((tokens // 2,) + block, BF16),
            pltpu.VMEM((devices // 2,) + block, BF16),
            pltpu.VMEM((tokens // 2,) + block, BF16),
            pltpu.VMEM((devices // 2,) + block, BF16),
            pltpu.VMEM((2 * sections + 1, pad, LANES), F32),
            pltpu.VMEM((2 * sections, 3, rank, LANES), F32),
            pltpu.VMEM(block, BF16),
            pltpu.VMEM((2, tokens // 2) + block, BF16),
            pltpu.VMEM((2, LANES), F32),
            pltpu.VMEM((devices // 2, 2, LANES), F32),
            pltpu.VMEM((2, 2, LANES), F32),
            pltpu.VMEM((2, tokens // 2, LANES), F32),
            pltpu.VMEM((tokens // 2, rows_dev), BF16),
            pltpu.VMEM((tokens // 2, rows_dev), BF16),
            pltpu.VMEM((tokens // 2,) + block, BF16),
            pltpu.VMEM((devices // 2,) + block, BF16),
            pltpu.VMEM(block, BF16),
            pltpu.VMEM((2, tokens // 2) + block, BF16),
            pltpu.VMEM((2 * rows_dev, dim), BF16),
            pltpu.SemaphoreType.DMA((SEMS,)),
            pltpu.SemaphoreType.DMA((SEMS,)),
        ],
        compiler_params=pltpu.CompilerParams(
            collective_id=0, has_side_effects=True, vmem_limit_bytes=48000000
        ),
        name="cascade",
    )(*[pltpu.with_memory_space_constraint(value, pltpu.HBM) for value in inputs])
    return pl.pallas_call(
        table_kernel,
        out_shape=(
            jax.ShapeDtypeStruct((batches, width), F32),
            jax.ShapeDtypeStruct((rows_dev, dim), BF16),
        ),
        in_specs=[hbm, vmem, vmem],
        out_specs=(hbm, hbm),
        scratch_shapes=[
            pltpu.VMEM((3 * tokens, dim), BF16),
            pltpu.VMEM((rows_dev, dim), BF16),
            pltpu.SemaphoreType.DMA,
            pltpu.SemaphoreType.DMA((4,)),
        ],
        compiler_params=pltpu.CompilerParams(vmem_limit_bytes=16000000),
        name="table_grad",
    )(token_loss, left, right)


def solution(mesh):
    return jax.shard_map(
        per_device,
        mesh=mesh,
        in_specs=(
            P(None, "dp"),
            P(None, "dp"),
            P(("section", "dp"), None),
            P(None, "section", None),
            P(None, "section", None, None),
            P(None, "section", None, None),
            P(),
        ),
        out_specs=(P(None, "dp"), P(("section", "dp"), None)),
        check_vma=False,
    )
```

```python
import functools
import math

import jax
import jax.numpy as jnp
import ml_dtypes
import numpy as np
from jax import lax
from jax.experimental import pallas as pl
from jax.experimental.pallas import tpu as pltpu
from jax.sharding import PartitionSpec as P

EPS = 1e-06
CAP = 30.0
GELU_C = 0.7978845608028654
LANES = 128
F32 = jnp.float32
BF16 = jnp.bfloat16
IDS, LOOK, HEAD, STAT, GRAD, EMB = range(6)
ACROSS, MATE, RELAY = 6, 8, 10
TABLE, GOAL, TABLE_MATE, HEAD_MATE, EMB_MATE, STAT_MATE, SCORE_MATE = range(12, 19)
OUT, IN, SEMS = 19, 25, 31


def gelu_tanh(values):
    return 0.5 * values * (1.0 + jnp.tanh(GELU_C * (values + 0.044715 * values * values * values)))


def gelu_slope(values):
    inner = jnp.tanh(GELU_C * (values + 0.044715 * values * values * values))
    return 0.5 * (1.0 + inner) + 0.5 * values * (1.0 - inner * inner) * GELU_C * (
        1.0 + 3.0 * 0.044715 * values * values
    )


def rounded(values):
    return values.astype(BF16).astype(F32)


def cascade(
    sections, replicas, per_dp, pad,
    rank, token_hbm, target_hbm, table_hbm, gain_hbm, fgain_hbm, win_hbm, wout_hbm,
    loss_hbm, left_ref, right_ref,
    token_ref, target_ref, gain_ref, fgain_ref, win_ref, wout_ref, loss_ref,
    ids_ref, idbuf, idrow, packed, gain_wide, first_wide, second_wide,
    flat, tok, look_out, look_in, goal_out, goal_in, layer_in, kept, head_out, head_in,
    stat_out, stat_in, stat_sum, score_out, score_in, grad_out, grad_in,
    emb_out, emb_in, table_ref, send_sem, recv_sem,
):
    devices = sections * replicas
    tokens = replicas * per_dp
    rows_dev = table_ref.shape[0] // 2
    dim = table_ref.shape[1]
    chunks = dim // LANES
    layers = 2 * sections
    scale_in = math.sqrt(dim)
    sec, rep = lax.axis_index("section"), lax.axis_index("dp")
    me = sec * replicas + rep
    all_own = per_dp == sections
    own = sec < per_dp
    own_half = per_dp // 2
    count_half = tokens // 2
    half = sections // 2
    group, side = sec // 2, sec % 2
    partner = sec + 1 - 2 * side
    side_me = group * replicas + rep
    my_half = rep * own_half + group
    if not all_own:
        my_half = jnp.where(own, my_half, -1)
    blocks = (pad // 8, 8, LANES)
    my_rows = pl.ds(pl.multiple_of(side * count_half, 16), count_half)
    mate_rows = pl.ds(pl.multiple_of((1 - side) * count_half, 16), count_half)

    def if_own(body):
        if all_own:
            body()
        else:
            pl.when(own)(body)

    def spread(phase, count, first, target, skip, src, dst, part=0, parts=1):
        def step(i, _):
            at = lax.rem(first + parts * i + part, count)

            @pl.when(at != skip)
            def _():
                pltpu.make_async_remote_copy(
                    src_ref=src(at),
                    dst_ref=dst,
                    send_sem=send_sem.at[phase],
                    recv_sem=recv_sem.at[phase],
                    device_id=target(at),
                    device_id_type=pl.DeviceIdType.MESH,
                ).start()

            @pl.when(at == skip)
            def _():
                pltpu.make_async_copy(src(at), dst, recv_sem.at[phase]).start()

            return 0

        lax.fori_loop(0, count // parts, step, 0, unroll=16)

    def take(ref, sem):
        pltpu.make_async_copy(ref, ref, sem).wait()

    def token_device(h):
        return (2 * (h % own_half) + side, h // own_half)

    def side_device(q):
        return (2 * (q // replicas) + side, q % replicas)

    def pair_copy(phase, src, dst):
        return pltpu.make_async_remote_copy(
            src_ref=src,
            dst_ref=dst,
            send_sem=send_sem.at[phase],
            recv_sem=recv_sem.at[phase],
            device_id=(partner, rep),
            device_id_type=pl.DeviceIdType.MESH,
        )

    barrier = pltpu.get_barrier_semaphore()

    def signal(target):
        pl.semaphore_signal(
            barrier, inc=1, device_id=target, device_id_type=pl.DeviceIdType.MESH
        )

    def greet(i, _):
        signal(side_device(lax.rem(side_me + 1 + i, devices // 2)))
        return 0

    lax.fori_loop(0, devices // 2 - 1, greet, 0, unroll=8)
    signal((partner, rep))
    inputs = [
        pltpu.make_async_copy(src, dst, recv_sem.at[IN + i])
        for i, (src, dst) in enumerate(
            (
                (token_hbm, token_ref),
                (target_hbm, target_ref),
                (win_hbm, win_ref),
                (wout_hbm, wout_ref),
                (gain_hbm, gain_ref),
                (fgain_hbm, fgain_ref),
            )
        )
    ]
    for move in inputs:
        move.start()
    own_table = table_ref.at[pl.ds(0, rows_dev)]
    load = pltpu.make_async_copy(table_hbm, own_table, recv_sem.at[TABLE])
    load.start()
    flat[...] = jnp.zeros_like(flat)
    tok[...] = jnp.zeros_like(tok)
    inputs[0].wait()
    inputs[1].wait()
    row = lax.broadcasted_iota(jnp.int32, (2 * per_dp, LANES), 0)
    made = jnp.zeros((2 * per_dp, LANES), jnp.int32)
    batches, width = token_ref.shape
    for b in range(batches):
        for w in range(width):
            k = b * width + w
            made = jnp.where(row == k, token_ref[b : b + 1, w : w + 1], made)
            made = jnp.where(row == per_dp + k, target_ref[b : b + 1, w : w + 1], made)
    ids_ref[...] = made
    for move in inputs[2:]:
        move.wait()

    def pack_row(values):
        for j in range(chunks):
            tok[j : j + 1, :] = values[:, j * LANES : (j + 1) * LANES]
        return tok[...]

    both_gains = gain_ref[...].astype(F32)
    for c in range(2):
        for slot, src in ((0, win_ref), (rank, wout_ref)):
            values = src[c, 0].astype(F32)
            for j in range(chunks):
                flat[pl.ds(j, rank, stride=pad), :] = values[:, j * LANES : (j + 1) * LANES]
            packed[c, side, group, pl.ds(slot, rank)] = (
                flat[pl.ds(0, rank * pad), :].reshape((rank,) + blocks).astype(BF16)
            )
        packed[c, side, group, 2 * rank] = (
            pack_row(both_gains[c : c + 1]).reshape(blocks).astype(BF16)
        )
    final_gain = pack_row(fgain_ref[...].astype(F32).reshape(1, dim))
    pl.semaphore_wait(barrier, devices // 2)

    spread(IDS, replicas, rep, lambda d: (sec, d), rep, lambda d: ids_ref, idbuf.at[rep])
    table_mate = pair_copy(TABLE_MATE, table_hbm, table_ref.at[pl.ds(rows_dev, rows_dev)])
    table_mate.start()

    def send_weights(phase, c, block, target):
        pltpu.make_async_remote_copy(
            src_ref=packed.at[c, side, block],
            dst_ref=packed.at[c, side, block],
            send_sem=send_sem.at[phase + c],
            recv_sem=recv_sem.at[phase + c],
            device_id=target,
            device_id_type=pl.DeviceIdType.MESH,
        ).start()

    def across(c):
        for i in range(1, half):
            send_weights(ACROSS, c, group, (2 * lax.rem(group + i, half) + side, rep))

    def relay_weights(c):
        if half > 1:
            take(packed.at[c, 0, pl.ds(0, half - 1)], recv_sem.at[ACROSS + c])
        for i in range(1, half):
            send_weights(RELAY, c, lax.rem(group + i, half), (partner, rep))

    def widen_weights(c):
        take(packed.at[c, 0, 0], recv_sem.at[MATE + c])
        if half > 1:
            take(packed.at[c, 0, pl.ds(0, half - 1)], recv_sem.at[RELAY + c])

        def widen(s, _):
            at = (c, s % 2, s // 2)
            gain = packed[at + (2 * rank,)].astype(F32)
            first = packed[at + (pl.ds(0, rank),)].astype(F32)
            gain_wide[c * sections + s] = gain.reshape(pad, LANES)
            second = packed[at + (pl.ds(rank, rank),)].astype(F32)
            first_wide[c * sections + s] = first.reshape(rank, pad, LANES)
            second_wide[c * sections + s] = second.reshape(rank, pad, LANES)
            return 0

        lax.fori_loop(0, sections, widen, 0)

    across(0)
    for c in range(2):
        send_weights(MATE, c, group, (partner, rep))

    take(idbuf, recv_sem.at[IDS])
    across(1)
    for d in range(replicas):
        for kind in range(2):
            for k in range(per_dp):
                at = (k % 2) * count_half + d * own_half + k // 2
                idrow[kind, pl.ds(at, 1), :] = idbuf[
                    d, pl.ds(kind * per_dp + k, 1), :
                ]
    wide = lambda value: jnp.concatenate([value] * (rows_dev // LANES), axis=1)
    both = lambda value: jnp.concatenate([wide(value)] * 2, axis=1)
    column = lax.broadcasted_iota(jnp.int32, (count_half, 2 * rows_dev), 1)
    column = column + jnp.where(
        column < rows_dev, me * rows_dev, (partner * replicas + rep - 1) * rows_dev
    )
    picked = both(idrow[0, my_rows, :]) == column
    load.wait()
    table_mate.wait_recv()

    def project(left, out, extra=()):
        for j in range(0, chunks, 2):
            part = jnp.dot(
                left, table_ref[:, j * LANES : (j + 2) * LANES], preferred_element_type=F32
            )
            flat[pl.ds(j, count_half, stride=pad), :] = part[:, :LANES]
            flat[pl.ds(j + 1, count_half, stride=pad), :] = part[:, LANES:]
        for q, values in enumerate(extra):
            flat[pl.ds(chunks + q, count_half, stride=pad), :] = values
        rows = flat[pl.ds(0, count_half * pad), :]
        out[...] = rows.reshape((count_half,) + blocks).astype(BF16)

    def send_rows(phase, out, into, part=0, parts=1):
        spread(
            phase, count_half, rep * own_half + group, token_device, my_half,
            lambda h: out.at[h], into.at[side_me], part, parts,
        )

    def total(into):
        return lax.fori_loop(
            0, devices // 2, lambda n, acc: acc + into[n].astype(F32),
            jnp.zeros(blocks, F32),
            unroll=4,
        ).reshape(pad, LANES)

    def whole(values):
        return jnp.sum(jnp.sum(values, axis=0, keepdims=True), axis=1, keepdims=True)

    def dots(values, rows):
        part = jnp.sum((values[None] * rows).reshape((rank,) + blocks), axis=1)
        return jnp.sum(jnp.sum(part, axis=1), axis=1, keepdims=True)

    def combine(weights, rows):
        wide_weights = jnp.broadcast_to(weights, (rank, LANES))
        acc = wide_weights[0:1] * rows[0]
        for k in range(1, rank):
            acc = acc + wide_weights[k : k + 1] * rows[k]
        return acc

    def norm_scale(x):
        return lax.rsqrt(whole(x * x) * (1.0 / dim) + EPS)

    def gather(phase, block, into):
        if_own(
            lambda: spread(
                phase, devices // 2, side_me, side_device, side_me,
                lambda n: block, into.at[side, my_half],
            )
        )

    def unpack(block, first, rows):
        flat[pl.ds(0, count_half * pad), :] = (
            block[...].astype(F32).reshape(count_half * pad, LANES)
        )
        for j in range(chunks):
            right_ref[first, rows, j * LANES : (j + 1) * LANES] = flat[
                pl.ds(j, count_half, stride=pad), :
            ].astype(BF16)

    project(jnp.where(picked, 1.0, 0.0).astype(BF16), look_out)
    send_rows(LOOK, look_out, look_in)
    mask = both(idrow[1, my_rows, :]) == column
    relay_weights(0)
    place = lax.broadcasted_iota(jnp.int32, (tokens, rows_dev), 1) + me * rows_dev
    chosen = jnp.where(wide(idrow[0]) == place, 1.0, 0.0)
    high_scale = float(np.float32(scale_in).astype(ml_dtypes.bfloat16))
    low_scale = float(np.float32(scale_in - high_scale).astype(ml_dtypes.bfloat16))
    left_ref[pl.ds(tokens, tokens), :] = (chosen * high_scale).astype(BF16)
    left_ref[pl.ds(2 * tokens, tokens), :] = (chosen * low_scale).astype(BF16)
    project(jnp.where(mask, 1.0, 0.0).astype(BF16), goal_out)
    relay_weights(1)
    widen_weights(0)
    widen_weights(1)

    if_own(lambda: take(look_in, recv_sem.at[LOOK]))
    send_rows(GOAL, goal_out, goal_in, 0, 2)

    def forward():
        x = rounded(total(look_in) * scale_in)

        def layer(index, x):
            layer_in[index] = x
            scale = norm_scale(x)
            pre = dots(rounded(x * scale * gain_wide[index]), first_wide[index])
            hidden = rounded(gelu_tanh(pre))
            kept[index, 0] = jnp.broadcast_to(scale, (rank, LANES))
            kept[index, 1] = jnp.broadcast_to(gelu_slope(pre), (rank, LANES))
            kept[index, 2] = jnp.broadcast_to(pre, (rank, LANES))
            return rounded(x + combine(hidden, second_wide[index]))

        x = lax.fori_loop(0, layers, layer, x, unroll=2)
        layer_in[layers] = x
        head_out[...] = (x * norm_scale(x) * final_gain).reshape(blocks).astype(BF16)

    if_own(forward)
    gather(HEAD, head_out, head_in)
    take(head_in.at[side], recv_sem.at[HEAD])
    head_mate = pair_copy(HEAD_MATE, head_in.at[side], head_in.at[side])
    head_mate.start()
    send_rows(GOAL, goal_out, goal_in, 1, 2)
    unpack(head_in.at[side], 0, my_rows)
    scores = lax.dot_general(
        right_ref[0, my_rows, :], table_ref[...], (((1,), (1,)), ((), ())),
        preferred_element_type=F32,
    )
    squash = jnp.tanh(scores / CAP)
    capped = CAP * squash
    powers = jnp.exp(capped)
    slope = 1.0 - squash * squash
    others = jnp.where(mask, 0.0, powers)
    exp_sum = jnp.sum(others, axis=1, keepdims=True)
    goal = jnp.sum(jnp.where(mask, capped, 0.0), axis=1, keepdims=True)
    lane = lax.broadcasted_iota(jnp.int32, (count_half, LANES), 1)
    here = lane == lax.broadcasted_iota(jnp.int32, (count_half, LANES), 0)
    stat_out[0:1, :] = jnp.sum(jnp.where(here, exp_sum, 0.0), axis=0, keepdims=True)
    stat_out[1:2, :] = jnp.sum(jnp.where(here, goal, 0.0), axis=0, keepdims=True)
    share = jnp.where(lane < LANES // 2, exp_sum, goal)
    high = rounded(share)
    middle = rounded(share - high)
    shares = (high, middle, rounded(share - high - middle))
    project((others * slope).astype(BF16), grad_out, shares)
    send_rows(GRAD, grad_out, grad_in)
    spread(
        STAT, devices // 2, side_me, side_device, side_me, lambda n: stat_out, stat_in.at[side_me]
    )

    def backward():
        take(grad_in, recv_sem.at[GRAD])
        take(goal_in, recv_sem.at[GOAL])
        goal_row = total(goal_in)
        sums = total(grad_in)
        share = sums[chunks : chunks + 1] + sums[chunks + 1 : chunks + 2]
        share = share + sums[chunks + 2 : chunks + 3]
        exp_others, goal = share[:, 0:1], share[:, LANES // 2 : LANES // 2 + 1]
        exp_total = exp_others + jnp.exp(goal)
        goal_squash = goal * (1.0 / CAP)
        goal_grad = rounded(-exp_others / exp_total * (1.0 - goal_squash * goal_squash))
        grad = sums * (1.0 / exp_total) + goal_row * goal_grad
        grad = grad * final_gain
        x = layer_in[layers]
        scale = norm_scale(x)
        normed = x * scale
        dy = rounded(scale * (grad - normed * (whole(grad * normed) * (1.0 / dim))))

        def layer(step, dy):
            index = layers - 1 - step
            scale = kept[index, 0][0:1, 0:1]
            pre_grad = rounded(dots(dy, second_wide[index]) * kept[index, 1][:, 0:1])
            mean = jnp.sum(pre_grad * kept[index, 2][:, 0:1], axis=0, keepdims=True)
            act_grad = combine(pre_grad, first_wide[index]) * gain_wide[index]
            back = act_grad - layer_in[index] * (scale * mean * (1.0 / dim))
            return rounded(dy + scale * back)

        dy = lax.fori_loop(0, layers, layer, dy, unroll=2)
        emb_out[...] = dy.reshape(blocks).astype(BF16)

    if_own(backward)
    gather(EMB, emb_out, emb_in)
    take(stat_in, recv_sem.at[STAT])
    tile = lax.fori_loop(
        0, devices // 2, lambda n, acc: acc + stat_in[n], jnp.zeros((2, LANES), F32), unroll=8
    )

    def column_of(kind):
        return jnp.broadcast_to(
            jnp.sum(jnp.where(here, tile[kind : kind + 1], 0.0), axis=1, keepdims=True),
            (count_half, LANES),
        )

    exp_others, goal = column_of(0), column_of(1)
    exp_total = exp_others + jnp.exp(goal)
    stat_sum[side] = tile
    stat_mate = pair_copy(STAT_MATE, stat_sum.at[side], stat_sum.at[side])
    stat_mate.start()
    score_grad = ((powers / both(exp_total) - jnp.where(mask, 1.0, 0.0)) * slope).astype(BF16)
    left_ref[my_rows, :] = score_grad[:, :rows_dev]
    score_out[...] = score_grad[:, rows_dev:]
    score_mate = pair_copy(SCORE_MATE, score_out, score_in)
    score_mate.start()
    head_mate.wait_recv()
    unpack(head_in.at[1 - side], 0, mate_rows)
    stat_mate.wait_recv()
    one = lax.broadcasted_iota(jnp.int32, (1, LANES), 1)
    for b in range(batches):
        for w in range(width):
            k = b * width + w
            sums = stat_sum[k % 2]
            losses = jnp.log(sums[0:1] + jnp.exp(sums[1:2])) - sums[1:2]
            loss_ref[b : b + 1, w : w + 1] = jnp.sum(
                jnp.where(one == rep * own_half + k // 2, losses, 0.0), axis=1, keepdims=True
            )
    score_mate.wait_recv()
    left_ref[mate_rows, :] = score_in[...]
    saves = [
        pltpu.make_async_copy(loss_ref, loss_hbm, recv_sem.at[OUT + 2]),
    ]
    for save in saves:
        save.start()

    take(emb_in.at[side], recv_sem.at[EMB])
    emb_mate = pair_copy(EMB_MATE, emb_in.at[side], emb_in.at[side])
    emb_mate.start()

    unpack(emb_in.at[side], 1, my_rows)
    emb_mate.wait_recv()
    unpack(emb_in.at[1 - side], 1, mate_rows)

    for move in (table_mate, head_mate, stat_mate, score_mate, emb_mate):
        move.wait_send()
    take(idbuf.at[pl.ds(0, replicas - 1)], send_sem.at[IDS])
    for c in range(2):
        take(packed.at[c, 0, 0], send_sem.at[MATE + c])
        if half > 1:
            take(packed.at[c, 0, pl.ds(0, half - 1)], send_sem.at[ACROSS + c])
            take(packed.at[c, 0, pl.ds(0, half - 1)], send_sem.at[RELAY + c])
    take(stat_in.at[pl.ds(0, devices // 2 - 1)], send_sem.at[STAT])
    sent = ((LOOK, look_out), (GOAL, goal_out), (GRAD, grad_out))

    def owned():
        for phase, out in sent:
            take(out.at[pl.ds(0, count_half - 1)], send_sem.at[phase])
        take(look_in.at[pl.ds(0, devices // 2 - 1)], send_sem.at[HEAD])
        take(grad_in.at[pl.ds(0, devices // 2 - 1)], send_sem.at[EMB])

    if_own(owned)
    if not all_own:

        @pl.when(jnp.logical_not(own))
        def _():
            for phase, out in sent:
                take(out, send_sem.at[phase])

    for save in saves:
        save.wait()


def table_kernel(loss_in, left_ref, right_ref, loss_out, out_hbm, right, out, sem, out_sem):
    tokens = right_ref.shape[1]
    steps = out_sem.shape[0]
    rows = out.shape[0] // steps
    moves = [pltpu.make_async_copy(loss_in, loss_out, sem)]
    moves[0].start()
    right[pl.ds(0, tokens), :] = right_ref[0]
    right[pl.ds(tokens, tokens), :] = right_ref[1]
    right[pl.ds(2 * tokens, tokens), :] = right_ref[1]
    across = left_ref[...].astype(F32).T.astype(BF16)
    for i in range(steps):
        at = pl.ds(i * rows, rows)
        out[at, :] = jnp.dot(
            across[i * rows : (i + 1) * rows], right[...], preferred_element_type=F32
        ).astype(BF16)
        save = pltpu.make_async_copy(out.at[at], out_hbm.at[at], out_sem.at[i])
        save.start()
        moves.append(save)
    for move in moves:
        move.wait()


def per_device(token_ids, target_ids, table, norm_gain, w_in, w_out, final_gain):
    sections, replicas = lax.axis_size("section"), lax.axis_size("dp")
    batches, width = token_ids.shape
    rows_dev, dim = table.shape
    rank = w_in.shape[2]
    per_dp = batches * width
    tokens = replicas * per_dp
    devices = sections * replicas
    chunks = dim // LANES
    pad = (chunks + 7) // 8 * 8
    assert per_dp <= sections and tokens % 32 == 0
    assert chunks % 2 == 0 and rows_dev % LANES == 0
    assert per_dp % 2 == 0 and sections % 2 == 0
    assert tokens <= LANES and pad >= chunks + 3
    block = (pad // 8, 8, LANES)
    vmem = pl.BlockSpec(memory_space=pltpu.VMEM)
    hbm = pl.BlockSpec(memory_space=pltpu.HBM)
    inputs = (token_ids, target_ids, table, norm_gain[:, 0], final_gain, w_in, w_out)
    token_loss, left, right = pl.pallas_call(
        functools.partial(cascade, sections, replicas, per_dp, pad, rank),
        out_shape=(
            jax.ShapeDtypeStruct((batches, width), F32),
            pltpu.VMEM((3 * tokens, rows_dev), BF16),
            pltpu.VMEM((2, tokens, dim), BF16),
        ),
        in_specs=[hbm] * 7,
        out_specs=(hbm, vmem, vmem),
        scratch_shapes=[
            pltpu.VMEM((batches, width), jnp.int32),
            pltpu.VMEM((batches, width), jnp.int32),
            pltpu.VMEM((2, dim), BF16),
            pltpu.VMEM((dim,), BF16),
            pltpu.VMEM((2, 1, rank, dim), BF16),
            pltpu.VMEM((2, 1, rank, dim), BF16),
            pltpu.VMEM((batches, width), F32),
            pltpu.VMEM((2 * per_dp, LANES), jnp.int32),
            pltpu.VMEM((replicas, 2 * per_dp, LANES), jnp.int32),
            pltpu.VMEM((2, tokens, LANES), jnp.int32),
            pltpu.VMEM((2, 2, sections // 2, 2 * rank + 1) + block, BF16),
            pltpu.VMEM((2 * sections, pad, LANES), F32),
            pltpu.VMEM((2 * sections, rank, pad, LANES), F32),
            pltpu.VMEM((2 * sections, rank, pad, LANES), F32),
            pltpu.VMEM((max(tokens // 2, rank) * pad, LANES), F32),
            pltpu.VMEM((pad, LANES), F32),
            pltpu.VMEM((tokens // 2,) + block, BF16),
            pltpu.VMEM((devices // 2,) + block, BF16),
            pltpu.VMEM((tokens // 2,) + block, BF16),
            pltpu.VMEM((devices // 2,) + block, BF16),
            pltpu.VMEM((2 * sections + 1, pad, LANES), F32),
            pltpu.VMEM((2 * sections, 3, rank, LANES), F32),
            pltpu.VMEM(block, BF16),
            pltpu.VMEM((2, tokens // 2) + block, BF16),
            pltpu.VMEM((2, LANES), F32),
            pltpu.VMEM((devices // 2, 2, LANES), F32),
            pltpu.VMEM((2, 2, LANES), F32),
            pltpu.VMEM((tokens // 2, rows_dev), BF16),
            pltpu.VMEM((tokens // 2, rows_dev), BF16),
            pltpu.VMEM((tokens // 2,) + block, BF16),
            pltpu.VMEM((devices // 2,) + block, BF16),
            pltpu.VMEM(block, BF16),
            pltpu.VMEM((2, tokens // 2) + block, BF16),
            pltpu.VMEM((2 * rows_dev, dim), BF16),
            pltpu.SemaphoreType.DMA((SEMS,)),
            pltpu.SemaphoreType.DMA((SEMS,)),
        ],
        compiler_params=pltpu.CompilerParams(
            collective_id=0, has_side_effects=True, vmem_limit_bytes=48000000
        ),
        name="cascade",
    )(*[pltpu.with_memory_space_constraint(value, pltpu.HBM) for value in inputs])
    return pl.pallas_call(
        table_kernel,
        out_shape=(
            jax.ShapeDtypeStruct((batches, width), F32),
            jax.ShapeDtypeStruct((rows_dev, dim), BF16),
        ),
        in_specs=[hbm, vmem, vmem],
        out_specs=(hbm, hbm),
        scratch_shapes=[
            pltpu.VMEM((3 * tokens, dim), BF16),
            pltpu.VMEM((rows_dev, dim), BF16),
            pltpu.SemaphoreType.DMA,
            pltpu.SemaphoreType.DMA((4,)),
        ],
        compiler_params=pltpu.CompilerParams(vmem_limit_bytes=16000000),
        name="table_grad",
    )(token_loss, left, right)


def solution(mesh):
    return jax.shard_map(
        per_device,
        mesh=mesh,
        in_specs=(
            P(None, "dp"),
            P(None, "dp"),
            P(("section", "dp"), None),
            P(None, "section", None),
            P(None, "section", None, None),
            P(None, "section", None, None),
            P(),
        ),
        out_specs=(P(None, "dp"), P(("section", "dp"), None)),
        check_vma=False,
    )
```

```python
import functools
import math

import jax
import jax.numpy as jnp
import ml_dtypes
import numpy as np
from jax import lax
from jax.experimental import pallas as pl
from jax.experimental.pallas import tpu as pltpu
from jax.sharding import PartitionSpec as P

EPS = 1e-06
CAP = 30.0
GELU_C = 0.7978845608028654
LANES = 128
F32 = jnp.float32
BF16 = jnp.bfloat16
IDS, LOOK, HEAD, STAT, GRAD, EMB = range(6)
ACROSS, MATE, RELAY = 6, 8, 10
TABLE, GOAL, TABLE_MATE, HEAD_MATE, EMB_MATE, STAT_MATE, SCORE_MATE = range(12, 19)
OUT, IN, SEMS = 19, 25, 31


def gelu_tanh(values):
    return 0.5 * values * (1.0 + jnp.tanh(GELU_C * (values + 0.044715 * values * values * values)))


def gelu_slope(values):
    inner = jnp.tanh(GELU_C * (values + 0.044715 * values * values * values))
    return 0.5 * (1.0 + inner) + 0.5 * values * (1.0 - inner * inner) * GELU_C * (
        1.0 + 3.0 * 0.044715 * values * values
    )


def rounded(values):
    return values.astype(BF16).astype(F32)


def cascade(
    sections, replicas, per_dp, pad,
    rank, token_hbm, target_hbm, table_hbm, gain_hbm, fgain_hbm, win_hbm, wout_hbm,
    loss_hbm, left_ref, right_ref,
    token_ref, target_ref, gain_ref, fgain_ref, win_ref, wout_ref, loss_ref,
    ids_ref, idbuf, idrow, packed, gain_wide, first_wide, second_wide,
    flat, tok, look_out, look_in, goal_out, goal_in, layer_in, kept, head_out, head_in,
    stat_out, stat_in, stat_sum, score_out, score_in, grad_out, grad_in,
    emb_out, emb_in, table_ref, send_sem, recv_sem,
):
    devices = sections * replicas
    tokens = replicas * per_dp
    rows_dev = table_ref.shape[0] // 2
    dim = table_ref.shape[1]
    chunks = dim // LANES
    layers = 2 * sections
    scale_in = math.sqrt(dim)
    sec, rep = lax.axis_index("section"), lax.axis_index("dp")
    me = sec * replicas + rep
    all_own = per_dp == sections
    own = sec < per_dp
    own_half = per_dp // 2
    count_half = tokens // 2
    half = sections // 2
    group, side = sec // 2, sec % 2
    partner = sec + 1 - 2 * side
    side_me = group * replicas + rep
    my_half = rep * own_half + group
    if not all_own:
        my_half = jnp.where(own, my_half, -1)
    blocks = (pad // 8, 8, LANES)
    my_rows = pl.ds(pl.multiple_of(side * count_half, 16), count_half)
    mate_rows = pl.ds(pl.multiple_of((1 - side) * count_half, 16), count_half)

    def if_own(body):
        if all_own:
            body()
        else:
            pl.when(own)(body)

    def spread(phase, count, first, target, skip, src, dst, part=0, parts=1):
        def step(i, _):
            at = lax.rem(first + parts * i + part, count)

            @pl.when(at != skip)
            def _():
                pltpu.make_async_remote_copy(
                    src_ref=src(at),
                    dst_ref=dst,
                    send_sem=send_sem.at[phase],
                    recv_sem=recv_sem.at[phase],
                    device_id=target(at),
                    device_id_type=pl.DeviceIdType.MESH,
                ).start()

            @pl.when(at == skip)
            def _():
                pltpu.make_async_copy(src(at), dst, recv_sem.at[phase]).start()

            return 0

        lax.fori_loop(0, count // parts, step, 0, unroll=16)

    def take(ref, sem):
        pltpu.make_async_copy(ref, ref, sem).wait()

    def token_device(h):
        return (2 * (h % own_half) + side, h // own_half)

    def side_device(q):
        return (2 * (q // replicas) + side, q % replicas)

    def pair_copy(phase, src, dst):
        return pltpu.make_async_remote_copy(
            src_ref=src,
            dst_ref=dst,
            send_sem=send_sem.at[phase],
            recv_sem=recv_sem.at[phase],
            device_id=(partner, rep),
            device_id_type=pl.DeviceIdType.MESH,
        )

    barrier = pltpu.get_barrier_semaphore()

    def signal(target):
        pl.semaphore_signal(
            barrier, inc=1, device_id=target, device_id_type=pl.DeviceIdType.MESH
        )

    def greet(i, _):
        signal(side_device(lax.rem(side_me + 1 + i, devices // 2)))
        return 0

    lax.fori_loop(0, devices // 2 - 1, greet, 0, unroll=8)
    signal((partner, rep))
    inputs = [
        pltpu.make_async_copy(src, dst, recv_sem.at[IN + i])
        for i, (src, dst) in enumerate(
            (
                (token_hbm, token_ref),
                (target_hbm, target_ref),
                (win_hbm, win_ref),
                (wout_hbm, wout_ref),
                (gain_hbm, gain_ref),
                (fgain_hbm, fgain_ref),
            )
        )
    ]
    for move in inputs:
        move.start()
    own_table = table_ref.at[pl.ds(0, rows_dev)]
    load = pltpu.make_async_copy(table_hbm, own_table, recv_sem.at[TABLE])
    load.start()
    flat[...] = jnp.zeros_like(flat)
    tok[...] = jnp.zeros_like(tok)
    inputs[0].wait()
    inputs[1].wait()
    row = lax.broadcasted_iota(jnp.int32, (2 * per_dp, LANES), 0)
    made = jnp.zeros((2 * per_dp, LANES), jnp.int32)
    batches, width = token_ref.shape
    for b in range(batches):
        for w in range(width):
            k = b * width + w
            made = jnp.where(row == k, token_ref[b : b + 1, w : w + 1], made)
            made = jnp.where(row == per_dp + k, target_ref[b : b + 1, w : w + 1], made)
    ids_ref[...] = made
    for move in inputs[2:]:
        move.wait()

    def pack_row(values):
        for j in range(chunks):
            tok[j : j + 1, :] = values[:, j * LANES : (j + 1) * LANES]
        return tok[...]

    both_gains = gain_ref[...].astype(F32)
    for c in range(2):
        for slot, src in ((0, win_ref), (rank, wout_ref)):
            values = src[c, 0].astype(F32)
            for j in range(chunks):
                flat[pl.ds(j, rank, stride=pad), :] = values[:, j * LANES : (j + 1) * LANES]
            packed[c, side, group, pl.ds(slot, rank)] = (
                flat[pl.ds(0, rank * pad), :].reshape((rank,) + blocks).astype(BF16)
            )
        packed[c, side, group, 2 * rank] = (
            pack_row(both_gains[c : c + 1]).reshape(blocks).astype(BF16)
        )
    final_gain = pack_row(fgain_ref[...].astype(F32).reshape(1, dim))
    pl.semaphore_wait(barrier, devices // 2)

    spread(IDS, replicas, rep, lambda d: (sec, d), rep, lambda d: ids_ref, idbuf.at[rep])
    table_mate = pair_copy(TABLE_MATE, table_hbm, table_ref.at[pl.ds(rows_dev, rows_dev)])
    table_mate.start()

    def send_weights(phase, c, block, target):
        pltpu.make_async_remote_copy(
            src_ref=packed.at[c, side, block],
            dst_ref=packed.at[c, side, block],
            send_sem=send_sem.at[phase + c],
            recv_sem=recv_sem.at[phase + c],
            device_id=target,
            device_id_type=pl.DeviceIdType.MESH,
        ).start()

    def across(c):
        for i in range(1, half):
            send_weights(ACROSS, c, group, (2 * lax.rem(group + i, half) + side, rep))

    def relay_weights(c):
        if half > 1:
            take(packed.at[c, 0, pl.ds(0, half - 1)], recv_sem.at[ACROSS + c])
        for i in range(1, half):
            send_weights(RELAY, c, lax.rem(group + i, half), (partner, rep))

    def widen_weights(c):
        take(packed.at[c, 0, 0], recv_sem.at[MATE + c])
        if half > 1:
            take(packed.at[c, 0, pl.ds(0, half - 1)], recv_sem.at[RELAY + c])

        def widen(s, _):
            at = (c, s % 2, s // 2)
            gain = packed[at + (2 * rank,)].astype(F32)
            first = packed[at + (pl.ds(0, rank),)].astype(F32)
            gain_wide[c * sections + s] = gain.reshape(pad, LANES)
            second = packed[at + (pl.ds(rank, rank),)].astype(F32)
            first_wide[c * sections + s] = first.reshape(rank, pad, LANES)
            second_wide[c * sections + s] = second.reshape(rank, pad, LANES)
            return 0

        lax.fori_loop(0, sections, widen, 0)

    across(0)
    for c in range(2):
        send_weights(MATE, c, group, (partner, rep))

    take(idbuf, recv_sem.at[IDS])
    across(1)
    for d in range(replicas):
        for kind in range(2):
            for k in range(per_dp):
                at = (k % 2) * count_half + d * own_half + k // 2
                idrow[kind, pl.ds(at, 1), :] = idbuf[
                    d, pl.ds(kind * per_dp + k, 1), :
                ]
    wide = lambda value: jnp.concatenate([value] * (rows_dev // LANES), axis=1)
    both = lambda value: jnp.concatenate([wide(value)] * 2, axis=1)
    column = lax.broadcasted_iota(jnp.int32, (count_half, 2 * rows_dev), 1)
    column = column + jnp.where(
        column < rows_dev, me * rows_dev, (partner * replicas + rep - 1) * rows_dev
    )
    picked = both(idrow[0, my_rows, :]) == column
    load.wait()
    table_mate.wait_recv()

    def project(left, out, extra=()):
        for j in range(0, chunks, 2):
            part = jnp.dot(
                left, table_ref[:, j * LANES : (j + 2) * LANES], preferred_element_type=F32
            )
            flat[pl.ds(j, count_half, stride=pad), :] = part[:, :LANES]
            flat[pl.ds(j + 1, count_half, stride=pad), :] = part[:, LANES:]
        for q, values in enumerate(extra):
            flat[pl.ds(chunks + q, count_half, stride=pad), :] = values
        rows = flat[pl.ds(0, count_half * pad), :]
        out[...] = rows.reshape((count_half,) + blocks).astype(BF16)

    def send_rows(phase, out, into, part=0, parts=1):
        spread(
            phase, count_half, rep * own_half + group, token_device, my_half,
            lambda h: out.at[h], into.at[side_me], part, parts,
        )

    def total(into):
        return lax.fori_loop(
            0, devices // 2, lambda n, acc: acc + into[n].astype(F32),
            jnp.zeros(blocks, F32),
            unroll=4,
        ).reshape(pad, LANES)

    def whole(values):
        return jnp.sum(jnp.sum(values, axis=0, keepdims=True), axis=1, keepdims=True)

    def dots(values, rows):
        part = jnp.sum((values[None] * rows).reshape((rank,) + blocks), axis=1)
        return jnp.sum(jnp.sum(part, axis=1), axis=1, keepdims=True)

    def wide_dots(values, rows):
        return jnp.broadcast_to(dots(values, rows), (rank, LANES))

    def combine(weights, rows):
        wide_weights = jnp.broadcast_to(weights, (rank, LANES))
        acc = wide_weights[0:1] * rows[0]
        for k in range(1, rank):
            acc = acc + wide_weights[k : k + 1] * rows[k]
        return acc

    def norm_scale(x):
        return lax.rsqrt(whole(x * x) * (1.0 / dim) + EPS)

    def gather(phase, block, into):
        if_own(
            lambda: spread(
                phase, devices // 2, side_me, side_device, side_me,
                lambda n: block, into.at[side, my_half],
            )
        )

    def unpack(block, first, rows):
        flat[pl.ds(0, count_half * pad), :] = (
            block[...].astype(F32).reshape(count_half * pad, LANES)
        )
        for j in range(chunks):
            right_ref[first, rows, j * LANES : (j + 1) * LANES] = flat[
                pl.ds(j, count_half, stride=pad), :
            ].astype(BF16)

    project(jnp.where(picked, 1.0, 0.0).astype(BF16), look_out)
    send_rows(LOOK, look_out, look_in)
    mask = both(idrow[1, my_rows, :]) == column
    relay_weights(0)
    place = lax.broadcasted_iota(jnp.int32, (tokens, rows_dev), 1) + me * rows_dev
    chosen = jnp.where(wide(idrow[0]) == place, 1.0, 0.0)
    high_scale = float(np.float32(scale_in).astype(ml_dtypes.bfloat16))
    low_scale = float(np.float32(scale_in - high_scale).astype(ml_dtypes.bfloat16))
    left_ref[pl.ds(tokens, tokens), :] = (chosen * high_scale).astype(BF16)
    left_ref[pl.ds(2 * tokens, tokens), :] = (chosen * low_scale).astype(BF16)
    project(jnp.where(mask, 1.0, 0.0).astype(BF16), goal_out)
    relay_weights(1)
    widen_weights(0)
    widen_weights(1)

    if_own(lambda: take(look_in, recv_sem.at[LOOK]))
    send_rows(GOAL, goal_out, goal_in, 0, 2)

    def forward():
        x = rounded(total(look_in) * scale_in)

        def layer(index, x):
            layer_in[index] = x
            scale = norm_scale(x)
            pre = wide_dots(rounded(x * scale * gain_wide[index]), first_wide[index])
            hidden = rounded(gelu_tanh(pre))
            kept[index, 0] = jnp.broadcast_to(scale, (rank, LANES))
            kept[index, 1] = jnp.broadcast_to(gelu_slope(pre), (rank, LANES))
            kept[index, 2] = jnp.broadcast_to(pre, (rank, LANES))
            return rounded(x + combine(hidden, second_wide[index]))

        x = lax.fori_loop(0, layers, layer, x, unroll=2)
        layer_in[layers] = x
        head_out[...] = (x * norm_scale(x) * final_gain).reshape(blocks).astype(BF16)

    if_own(forward)
    gather(HEAD, head_out, head_in)
    take(head_in.at[side], recv_sem.at[HEAD])
    head_mate = pair_copy(HEAD_MATE, head_in.at[side], head_in.at[side])
    head_mate.start()
    send_rows(GOAL, goal_out, goal_in, 1, 2)
    unpack(head_in.at[side], 0, my_rows)
    scores = lax.dot_general(
        right_ref[0, my_rows, :], table_ref[...], (((1,), (1,)), ((), ())),
        preferred_element_type=F32,
    )
    squash = jnp.tanh(scores / CAP)
    capped = CAP * squash
    powers = jnp.exp(capped)
    slope = 1.0 - squash * squash
    others = jnp.where(mask, 0.0, powers)
    exp_sum = jnp.sum(others, axis=1, keepdims=True)
    goal = jnp.sum(jnp.where(mask, capped, 0.0), axis=1, keepdims=True)
    lane = lax.broadcasted_iota(jnp.int32, (count_half, LANES), 1)
    here = lane == lax.broadcasted_iota(jnp.int32, (count_half, LANES), 0)
    stat_out[0:1, :] = jnp.sum(jnp.where(here, exp_sum, 0.0), axis=0, keepdims=True)
    stat_out[1:2, :] = jnp.sum(jnp.where(here, goal, 0.0), axis=0, keepdims=True)
    share = jnp.where(lane < LANES // 2, exp_sum, goal)
    high = rounded(share)
    middle = rounded(share - high)
    shares = (high, middle, rounded(share - high - middle))
    project((others * slope).astype(BF16), grad_out, shares)
    send_rows(GRAD, grad_out, grad_in)
    spread(
        STAT, devices // 2, side_me, side_device, side_me, lambda n: stat_out, stat_in.at[side_me]
    )

    def backward():
        take(grad_in, recv_sem.at[GRAD])
        take(goal_in, recv_sem.at[GOAL])
        goal_row = total(goal_in)
        sums = total(grad_in)
        share = sums[chunks : chunks + 1] + sums[chunks + 1 : chunks + 2]
        share = share + sums[chunks + 2 : chunks + 3]
        exp_others, goal = share[:, 0:1], share[:, LANES // 2 : LANES // 2 + 1]
        exp_total = exp_others + jnp.exp(goal)
        goal_squash = goal * (1.0 / CAP)
        goal_grad = rounded(-exp_others / exp_total * (1.0 - goal_squash * goal_squash))
        grad = sums * (1.0 / exp_total) + goal_row * goal_grad
        grad = grad * final_gain
        x = layer_in[layers]
        scale = norm_scale(x)
        normed = x * scale
        dy = rounded(scale * (grad - normed * (whole(grad * normed) * (1.0 / dim))))

        def layer(step, dy):
            index = layers - 1 - step
            scale = kept[index, 0][0:1]
            hidden_grad = wide_dots(dy, second_wide[index])
            pre_grad = rounded(hidden_grad * kept[index, 1])
            mean = jnp.sum(pre_grad * kept[index, 2], axis=0, keepdims=True)
            act_grad = combine(pre_grad, first_wide[index]) * gain_wide[index]
            back = act_grad - layer_in[index] * (scale * mean * (1.0 / dim))
            return rounded(dy + scale * back)

        dy = lax.fori_loop(0, layers, layer, dy, unroll=2)
        emb_out[...] = dy.reshape(blocks).astype(BF16)

    if_own(backward)
    gather(EMB, emb_out, emb_in)
    take(stat_in, recv_sem.at[STAT])
    tile = lax.fori_loop(
        0, devices // 2, lambda n, acc: acc + stat_in[n], jnp.zeros((2, LANES), F32), unroll=8
    )

    def column_of(kind):
        return jnp.broadcast_to(
            jnp.sum(jnp.where(here, tile[kind : kind + 1], 0.0), axis=1, keepdims=True),
            (count_half, LANES),
        )

    exp_others, goal = column_of(0), column_of(1)
    exp_total = exp_others + jnp.exp(goal)
    stat_sum[side] = tile
    stat_mate = pair_copy(STAT_MATE, stat_sum.at[side], stat_sum.at[side])
    stat_mate.start()
    score_grad = ((powers / both(exp_total) - jnp.where(mask, 1.0, 0.0)) * slope).astype(BF16)
    left_ref[my_rows, :] = score_grad[:, :rows_dev]
    score_out[...] = score_grad[:, rows_dev:]
    score_mate = pair_copy(SCORE_MATE, score_out, score_in)
    score_mate.start()
    head_mate.wait_recv()
    unpack(head_in.at[1 - side], 0, mate_rows)
    stat_mate.wait_recv()
    one = lax.broadcasted_iota(jnp.int32, (1, LANES), 1)
    for b in range(batches):
        for w in range(width):
            k = b * width + w
            sums = stat_sum[k % 2]
            losses = jnp.log(sums[0:1] + jnp.exp(sums[1:2])) - sums[1:2]
            loss_ref[b : b + 1, w : w + 1] = jnp.sum(
                jnp.where(one == rep * own_half + k // 2, losses, 0.0), axis=1, keepdims=True
            )
    score_mate.wait_recv()
    left_ref[mate_rows, :] = score_in[...]
    saves = [
        pltpu.make_async_copy(loss_ref, loss_hbm, recv_sem.at[OUT + 2]),
    ]
    for save in saves:
        save.start()

    take(emb_in.at[side], recv_sem.at[EMB])
    emb_mate = pair_copy(EMB_MATE, emb_in.at[side], emb_in.at[side])
    emb_mate.start()

    unpack(emb_in.at[side], 1, my_rows)
    emb_mate.wait_recv()
    unpack(emb_in.at[1 - side], 1, mate_rows)

    for move in (table_mate, head_mate, stat_mate, score_mate, emb_mate):
        move.wait_send()
    take(idbuf.at[pl.ds(0, replicas - 1)], send_sem.at[IDS])
    for c in range(2):
        take(packed.at[c, 0, 0], send_sem.at[MATE + c])
        if half > 1:
            take(packed.at[c, 0, pl.ds(0, half - 1)], send_sem.at[ACROSS + c])
            take(packed.at[c, 0, pl.ds(0, half - 1)], send_sem.at[RELAY + c])
    take(stat_in.at[pl.ds(0, devices // 2 - 1)], send_sem.at[STAT])
    sent = ((LOOK, look_out), (GOAL, goal_out), (GRAD, grad_out))

    def owned():
        for phase, out in sent:
            take(out.at[pl.ds(0, count_half - 1)], send_sem.at[phase])
        take(look_in.at[pl.ds(0, devices // 2 - 1)], send_sem.at[HEAD])
        take(grad_in.at[pl.ds(0, devices // 2 - 1)], send_sem.at[EMB])

    if_own(owned)
    if not all_own:

        @pl.when(jnp.logical_not(own))
        def _():
            for phase, out in sent:
                take(out, send_sem.at[phase])

    for save in saves:
        save.wait()


def table_kernel(loss_in, left_ref, right_ref, loss_out, out_hbm, right, out, sem, out_sem):
    tokens = right_ref.shape[1]
    steps = out_sem.shape[0]
    rows = out.shape[0] // steps
    moves = [pltpu.make_async_copy(loss_in, loss_out, sem)]
    moves[0].start()
    right[pl.ds(0, tokens), :] = right_ref[0]
    right[pl.ds(tokens, tokens), :] = right_ref[1]
    right[pl.ds(2 * tokens, tokens), :] = right_ref[1]
    across = left_ref[...].astype(F32).T.astype(BF16)
    for i in range(steps):
        at = pl.ds(i * rows, rows)
        out[at, :] = jnp.dot(
            across[i * rows : (i + 1) * rows], right[...], preferred_element_type=F32
        ).astype(BF16)
        save = pltpu.make_async_copy(out.at[at], out_hbm.at[at], out_sem.at[i])
        save.start()
        moves.append(save)
    for move in moves:
        move.wait()


def per_device(token_ids, target_ids, table, norm_gain, w_in, w_out, final_gain):
    sections, replicas = lax.axis_size("section"), lax.axis_size("dp")
    batches, width = token_ids.shape
    rows_dev, dim = table.shape
    rank = w_in.shape[2]
    per_dp = batches * width
    tokens = replicas * per_dp
    devices = sections * replicas
    chunks = dim // LANES
    pad = (chunks + 7) // 8 * 8
    assert per_dp <= sections and tokens % 32 == 0
    assert chunks % 2 == 0 and rows_dev % LANES == 0
    assert per_dp % 2 == 0 and sections % 2 == 0
    assert tokens <= LANES and pad >= chunks + 3
    block = (pad // 8, 8, LANES)
    vmem = pl.BlockSpec(memory_space=pltpu.VMEM)
    hbm = pl.BlockSpec(memory_space=pltpu.HBM)
    inputs = (token_ids, target_ids, table, norm_gain[:, 0], final_gain, w_in, w_out)
    token_loss, left, right = pl.pallas_call(
        functools.partial(cascade, sections, replicas, per_dp, pad, rank),
        out_shape=(
            jax.ShapeDtypeStruct((batches, width), F32),
            pltpu.VMEM((3 * tokens, rows_dev), BF16),
            pltpu.VMEM((2, tokens, dim), BF16),
        ),
        in_specs=[hbm] * 7,
        out_specs=(hbm, vmem, vmem),
        scratch_shapes=[
            pltpu.VMEM((batches, width), jnp.int32),
            pltpu.VMEM((batches, width), jnp.int32),
            pltpu.VMEM((2, dim), BF16),
            pltpu.VMEM((dim,), BF16),
            pltpu.VMEM((2, 1, rank, dim), BF16),
            pltpu.VMEM((2, 1, rank, dim), BF16),
            pltpu.VMEM((batches, width), F32),
            pltpu.VMEM((2 * per_dp, LANES), jnp.int32),
            pltpu.VMEM((replicas, 2 * per_dp, LANES), jnp.int32),
            pltpu.VMEM((2, tokens, LANES), jnp.int32),
            pltpu.VMEM((2, 2, sections // 2, 2 * rank + 1) + block, BF16),
            pltpu.VMEM((2 * sections, pad, LANES), F32),
            pltpu.VMEM((2 * sections, rank, pad, LANES), F32),
            pltpu.VMEM((2 * sections, rank, pad, LANES), F32),
            pltpu.VMEM((max(tokens // 2, rank) * pad, LANES), F32),
            pltpu.VMEM((pad, LANES), F32),
            pltpu.VMEM((tokens // 2,) + block, BF16),
            pltpu.VMEM((devices // 2,) + block, BF16),
            pltpu.VMEM((tokens // 2,) + block, BF16),
            pltpu.VMEM((devices // 2,) + block, BF16),
            pltpu.VMEM((2 * sections + 1, pad, LANES), F32),
            pltpu.VMEM((2 * sections, 3, rank, LANES), F32),
            pltpu.VMEM(block, BF16),
            pltpu.VMEM((2, tokens // 2) + block, BF16),
            pltpu.VMEM((2, LANES), F32),
            pltpu.VMEM((devices // 2, 2, LANES), F32),
            pltpu.VMEM((2, 2, LANES), F32),
            pltpu.VMEM((tokens // 2, rows_dev), BF16),
            pltpu.VMEM((tokens // 2, rows_dev), BF16),
            pltpu.VMEM((tokens // 2,) + block, BF16),
            pltpu.VMEM((devices // 2,) + block, BF16),
            pltpu.VMEM(block, BF16),
            pltpu.VMEM((2, tokens // 2) + block, BF16),
            pltpu.VMEM((2 * rows_dev, dim), BF16),
            pltpu.SemaphoreType.DMA((SEMS,)),
            pltpu.SemaphoreType.DMA((SEMS,)),
        ],
        compiler_params=pltpu.CompilerParams(
            collective_id=0, has_side_effects=True, vmem_limit_bytes=48000000
        ),
        name="cascade",
    )(*[pltpu.with_memory_space_constraint(value, pltpu.HBM) for value in inputs])
    return pl.pallas_call(
        table_kernel,
        out_shape=(
            jax.ShapeDtypeStruct((batches, width), F32),
            jax.ShapeDtypeStruct((rows_dev, dim), BF16),
        ),
        in_specs=[hbm, vmem, vmem],
        out_specs=(hbm, hbm),
        scratch_shapes=[
            pltpu.VMEM((3 * tokens, dim), BF16),
            pltpu.VMEM((rows_dev, dim), BF16),
            pltpu.SemaphoreType.DMA,
            pltpu.SemaphoreType.DMA((4,)),
        ],
        compiler_params=pltpu.CompilerParams(vmem_limit_bytes=16000000),
        name="table_grad",
    )(token_loss, left, right)


def solution(mesh):
    return jax.shard_map(
        per_device,
        mesh=mesh,
        in_specs=(
            P(None, "dp"),
            P(None, "dp"),
            P(("section", "dp"), None),
            P(None, "section", None),
            P(None, "section", None, None),
            P(None, "section", None, None),
            P(),
        ),
        out_specs=(P(None, "dp"), P(("section", "dp"), None)),
        check_vma=False,
    )
```

```python
import functools
import math

import jax
import jax.numpy as jnp
import ml_dtypes
import numpy as np
from jax import lax
from jax.experimental import pallas as pl
from jax.experimental.pallas import tpu as pltpu
from jax.sharding import PartitionSpec as P

EPS = 1e-06
CAP = 30.0
GELU_C = 0.7978845608028654
LANES = 128
F32 = jnp.float32
BF16 = jnp.bfloat16
IDS, LOOK, HEAD, STAT, GRAD, EMB = range(6)
ACROSS, MATE, RELAY = 6, 8, 10
TABLE, GOAL, TABLE_MATE, HEAD_MATE, EMB_MATE, STAT_MATE, SCORE_MATE = range(12, 19)
OUT, IN, SEMS = 19, 25, 31


def gelu_tanh(values):
    return 0.5 * values * (1.0 + jnp.tanh(GELU_C * (values + 0.044715 * values * values * values)))


def gelu_slope(values):
    inner = jnp.tanh(GELU_C * (values + 0.044715 * values * values * values))
    return 0.5 * (1.0 + inner) + 0.5 * values * (1.0 - inner * inner) * GELU_C * (
        1.0 + 3.0 * 0.044715 * values * values
    )


def rounded(values):
    return values.astype(BF16).astype(F32)


def cascade(
    sections, replicas, per_dp, pad,
    rank, token_hbm, target_hbm, table_hbm, gain_hbm, fgain_hbm, win_hbm, wout_hbm,
    loss_hbm, left_ref, right_ref,
    token_ref, target_ref, gain_ref, fgain_ref, win_ref, wout_ref, loss_ref,
    ids_ref, idbuf, idrow, packed, gain_wide, first_wide, second_wide,
    flat, tok, look_out, look_in, goal_out, goal_in, layer_in, kept, head_out, head_in,
    stat_out, stat_in, stat_sum, score_out, score_in, grad_out, grad_in,
    emb_out, emb_in, table_ref, send_sem, recv_sem,
):
    devices = sections * replicas
    tokens = replicas * per_dp
    rows_dev = table_ref.shape[0] // 2
    dim = table_ref.shape[1]
    chunks = dim // LANES
    layers = 2 * sections
    scale_in = math.sqrt(dim)
    sec, rep = lax.axis_index("section"), lax.axis_index("dp")
    me = sec * replicas + rep
    all_own = per_dp == sections
    own = sec < per_dp
    own_half = per_dp // 2
    count_half = tokens // 2
    half = sections // 2
    group, side = sec // 2, sec % 2
    partner = sec + 1 - 2 * side
    side_me = group * replicas + rep
    my_half = rep * own_half + group
    if not all_own:
        my_half = jnp.where(own, my_half, -1)
    blocks = (pad // 8, 8, LANES)
    my_rows = pl.ds(pl.multiple_of(side * count_half, 16), count_half)
    mate_rows = pl.ds(pl.multiple_of((1 - side) * count_half, 16), count_half)

    def if_own(body):
        if all_own:
            body()
        else:
            pl.when(own)(body)

    def spread(phase, count, first, target, skip, src, dst, part=0, parts=1):
        def step(i, _):
            at = lax.rem(first + parts * i + part, count)

            @pl.when(at != skip)
            def _():
                pltpu.make_async_remote_copy(
                    src_ref=src(at),
                    dst_ref=dst,
                    send_sem=send_sem.at[phase],
                    recv_sem=recv_sem.at[phase],
                    device_id=target(at),
                    device_id_type=pl.DeviceIdType.MESH,
                ).start()

            @pl.when(at == skip)
            def _():
                pltpu.make_async_copy(src(at), dst, recv_sem.at[phase]).start()

            return 0

        lax.fori_loop(0, count // parts, step, 0, unroll=16)

    def take(ref, sem):
        pltpu.make_async_copy(ref, ref, sem).wait()

    def token_device(h):
        return (2 * (h % own_half) + side, h // own_half)

    def side_device(q):
        return (2 * (q // replicas) + side, q % replicas)

    def pair_copy(phase, src, dst):
        return pltpu.make_async_remote_copy(
            src_ref=src,
            dst_ref=dst,
            send_sem=send_sem.at[phase],
            recv_sem=recv_sem.at[phase],
            device_id=(partner, rep),
            device_id_type=pl.DeviceIdType.MESH,
        )

    barrier = pltpu.get_barrier_semaphore()

    def signal(target):
        pl.semaphore_signal(
            barrier, inc=1, device_id=target, device_id_type=pl.DeviceIdType.MESH
        )

    def greet(i, _):
        signal(side_device(lax.rem(side_me + 1 + i, devices // 2)))
        return 0

    lax.fori_loop(0, devices // 2 - 1, greet, 0, unroll=True)
    signal((partner, rep))
    inputs = [
        pltpu.make_async_copy(src, dst, recv_sem.at[IN + i])
        for i, (src, dst) in enumerate(
            (
                (token_hbm, token_ref),
                (target_hbm, target_ref),
                (win_hbm, win_ref),
                (wout_hbm, wout_ref),
                (gain_hbm, gain_ref),
                (fgain_hbm, fgain_ref),
            )
        )
    ]
    for move in inputs:
        move.start()
    own_table = table_ref.at[pl.ds(0, rows_dev)]
    load = pltpu.make_async_copy(table_hbm, own_table, recv_sem.at[TABLE])
    load.start()
    flat[...] = jnp.zeros_like(flat)
    tok[...] = jnp.zeros_like(tok)
    inputs[0].wait()
    inputs[1].wait()
    row = lax.broadcasted_iota(jnp.int32, (2 * per_dp, LANES), 0)
    made = jnp.zeros((2 * per_dp, LANES), jnp.int32)
    batches, width = token_ref.shape
    for b in range(batches):
        for w in range(width):
            k = b * width + w
            made = jnp.where(row == k, token_ref[b : b + 1, w : w + 1], made)
            made = jnp.where(row == per_dp + k, target_ref[b : b + 1, w : w + 1], made)
    ids_ref[...] = made
    for move in inputs[2:]:
        move.wait()

    def pack_row(values):
        for j in range(chunks):
            tok[j : j + 1, :] = values[:, j * LANES : (j + 1) * LANES]
        return tok[...]

    both_gains = gain_ref[...].astype(F32)
    for c in range(2):
        for slot, src in ((0, win_ref), (rank, wout_ref)):
            values = src[c, 0].astype(F32)
            for j in range(chunks):
                flat[pl.ds(j, rank, stride=pad), :] = values[:, j * LANES : (j + 1) * LANES]
            packed[c, side, group, pl.ds(slot, rank)] = (
                flat[pl.ds(0, rank * pad), :].reshape((rank,) + blocks).astype(BF16)
            )
        packed[c, side, group, 2 * rank] = (
            pack_row(both_gains[c : c + 1]).reshape(blocks).astype(BF16)
        )
    final_gain = pack_row(fgain_ref[...].astype(F32).reshape(1, dim))
    pl.semaphore_wait(barrier, devices // 2)

    spread(IDS, replicas, rep, lambda d: (sec, d), rep, lambda d: ids_ref, idbuf.at[rep])
    table_mate = pair_copy(TABLE_MATE, table_hbm, table_ref.at[pl.ds(rows_dev, rows_dev)])
    table_mate.start()

    def send_weights(phase, c, block, target):
        pltpu.make_async_remote_copy(
            src_ref=packed.at[c, side, block],
            dst_ref=packed.at[c, side, block],
            send_sem=send_sem.at[phase + c],
            recv_sem=recv_sem.at[phase + c],
            device_id=target,
            device_id_type=pl.DeviceIdType.MESH,
        ).start()

    def across(c):
        for i in range(1, half):
            send_weights(ACROSS, c, group, (2 * lax.rem(group + i, half) + side, rep))

    def relay_weights(c):
        if half > 1:
            take(packed.at[c, 0, pl.ds(0, half - 1)], recv_sem.at[ACROSS + c])
        for i in range(1, half):
            send_weights(RELAY, c, lax.rem(group + i, half), (partner, rep))

    def widen_weights(c):
        take(packed.at[c, 0, 0], recv_sem.at[MATE + c])
        if half > 1:
            take(packed.at[c, 0, pl.ds(0, half - 1)], recv_sem.at[RELAY + c])

        def widen(s, _):
            at = (c, s % 2, s // 2)
            gain = packed[at + (2 * rank,)].astype(F32)
            first = packed[at + (pl.ds(0, rank),)].astype(F32)
            gain_wide[c * sections + s] = gain.reshape(pad, LANES)
            second = packed[at + (pl.ds(rank, rank),)].astype(F32)
            first_wide[c * sections + s] = first.reshape(rank, pad, LANES)
            second_wide[c * sections + s] = second.reshape(rank, pad, LANES)
            return 0

        lax.fori_loop(0, sections, widen, 0)

    across(0)
    for c in range(2):
        send_weights(MATE, c, group, (partner, rep))

    take(idbuf, recv_sem.at[IDS])
    across(1)
    for d in range(replicas):
        for kind in range(2):
            for k in range(per_dp):
                at = (k % 2) * count_half + d * own_half + k // 2
                idrow[kind, pl.ds(at, 1), :] = idbuf[
                    d, pl.ds(kind * per_dp + k, 1), :
                ]
    wide = lambda value: jnp.concatenate([value] * (rows_dev // LANES), axis=1)
    both = lambda value: jnp.concatenate([wide(value)] * 2, axis=1)
    column = lax.broadcasted_iota(jnp.int32, (count_half, 2 * rows_dev), 1)
    column = column + jnp.where(
        column < rows_dev, me * rows_dev, (partner * replicas + rep - 1) * rows_dev
    )
    picked = both(idrow[0, my_rows, :]) == column
    load.wait()
    table_mate.wait_recv()

    def project(left, out, extra=()):
        for j in range(0, chunks, 2):
            part = jnp.dot(
                left, table_ref[:, j * LANES : (j + 2) * LANES], preferred_element_type=F32
            )
            flat[pl.ds(j, count_half, stride=pad), :] = part[:, :LANES]
            flat[pl.ds(j + 1, count_half, stride=pad), :] = part[:, LANES:]
        for q, values in enumerate(extra):
            flat[pl.ds(chunks + q, count_half, stride=pad), :] = values
        rows = flat[pl.ds(0, count_half * pad), :]
        out[...] = rows.reshape((count_half,) + blocks).astype(BF16)

    def send_rows(phase, out, into, part=0, parts=1):
        spread(
            phase, count_half, rep * own_half + group, token_device, my_half,
            lambda h: out.at[h], into.at[side_me], part, parts,
        )

    def total(into):
        return lax.fori_loop(
            0, devices // 2, lambda n, acc: acc + into[n].astype(F32),
            jnp.zeros(blocks, F32),
            unroll=16,
        ).reshape(pad, LANES)

    def whole(values):
        return jnp.sum(jnp.sum(values, axis=0, keepdims=True), axis=1, keepdims=True)

    def dots(values, rows):
        part = jnp.sum((values[None] * rows).reshape((rank,) + blocks), axis=1)
        return jnp.sum(jnp.sum(part, axis=1), axis=1, keepdims=True)

    def wide_dots(values, rows):
        return jnp.broadcast_to(dots(values, rows), (rank, LANES))

    def combine(weights, rows):
        wide_weights = jnp.broadcast_to(weights, (rank, LANES))
        acc = wide_weights[0:1] * rows[0]
        for k in range(1, rank):
            acc = acc + wide_weights[k : k + 1] * rows[k]
        return acc

    def norm_scale(x):
        return lax.rsqrt(whole(x * x) * (1.0 / dim) + EPS)

    def gather(phase, block, into):
        if_own(
            lambda: spread(
                phase, devices // 2, side_me, side_device, side_me,
                lambda n: block, into.at[side, my_half],
            )
        )

    def unpack(block, first, rows):
        flat[pl.ds(0, count_half * pad), :] = (
            block[...].astype(F32).reshape(count_half * pad, LANES)
        )
        for j in range(chunks):
            right_ref[first, rows, j * LANES : (j + 1) * LANES] = flat[
                pl.ds(j, count_half, stride=pad), :
            ].astype(BF16)

    project(jnp.where(picked, 1.0, 0.0).astype(BF16), look_out)
    send_rows(LOOK, look_out, look_in)
    mask = both(idrow[1, my_rows, :]) == column
    relay_weights(0)
    place = lax.broadcasted_iota(jnp.int32, (tokens, rows_dev), 1) + me * rows_dev
    chosen = jnp.where(wide(idrow[0]) == place, 1.0, 0.0)
    high_scale = float(np.float32(scale_in).astype(ml_dtypes.bfloat16))
    low_scale = float(np.float32(scale_in - high_scale).astype(ml_dtypes.bfloat16))
    left_ref[pl.ds(tokens, tokens), :] = (chosen * high_scale).astype(BF16)
    left_ref[pl.ds(2 * tokens, tokens), :] = (chosen * low_scale).astype(BF16)
    project(jnp.where(mask, 1.0, 0.0).astype(BF16), goal_out)
    relay_weights(1)
    widen_weights(0)
    widen_weights(1)
    send_rows(GOAL, goal_out, goal_in, 0, 4)

    if_own(lambda: take(look_in, recv_sem.at[LOOK]))
    send_rows(GOAL, goal_out, goal_in, 1, 4)

    def forward():
        x = rounded(total(look_in) * scale_in)

        def layer(index, x):
            layer_in[index] = x
            scale = norm_scale(x)
            pre = wide_dots(rounded(x * scale * gain_wide[index]), first_wide[index])
            hidden = rounded(gelu_tanh(pre))
            kept[index, 0] = jnp.broadcast_to(scale, (rank, LANES))
            kept[index, 1] = jnp.broadcast_to(gelu_slope(pre), (rank, LANES))
            kept[index, 2] = jnp.broadcast_to(pre, (rank, LANES))
            return rounded(x + combine(hidden, second_wide[index]))

        x = lax.fori_loop(0, layers, layer, x, unroll=2)
        layer_in[layers] = x
        head_out[...] = (x * norm_scale(x) * final_gain).reshape(blocks).astype(BF16)

    if_own(forward)
    gather(HEAD, head_out, head_in)
    take(head_in.at[side], recv_sem.at[HEAD])
    head_mate = pair_copy(HEAD_MATE, head_in.at[side], head_in.at[side])
    head_mate.start()
    send_rows(GOAL, goal_out, goal_in, 2, 4)
    send_rows(GOAL, goal_out, goal_in, 3, 4)
    unpack(head_in.at[side], 0, my_rows)
    scores = lax.dot_general(
        right_ref[0, my_rows, :], table_ref[...], (((1,), (1,)), ((), ())),
        preferred_element_type=F32,
    )
    squash = jnp.tanh(scores / CAP)
    capped = CAP * squash
    powers = jnp.exp(capped)
    slope = 1.0 - squash * squash
    others = jnp.where(mask, 0.0, powers)
    exp_sum = jnp.sum(others, axis=1, keepdims=True)
    goal = jnp.sum(jnp.where(mask, capped, 0.0), axis=1, keepdims=True)
    lane = lax.broadcasted_iota(jnp.int32, (count_half, LANES), 1)
    here = lane == lax.broadcasted_iota(jnp.int32, (count_half, LANES), 0)
    stat_out[0:1, :] = jnp.sum(jnp.where(here, exp_sum, 0.0), axis=0, keepdims=True)
    stat_out[1:2, :] = jnp.sum(jnp.where(here, goal, 0.0), axis=0, keepdims=True)
    share = jnp.where(lane < LANES // 2, exp_sum, goal)
    high = rounded(share)
    middle = rounded(share - high)
    shares = (high, middle, rounded(share - high - middle))
    project((others * slope).astype(BF16), grad_out, shares)
    send_rows(GRAD, grad_out, grad_in)
    spread(
        STAT, devices // 2, side_me, side_device, side_me, lambda n: stat_out, stat_in.at[side_me]
    )

    def backward():
        take(grad_in, recv_sem.at[GRAD])
        take(goal_in, recv_sem.at[GOAL])
        goal_row = total(goal_in)
        sums = total(grad_in)
        share = sums[chunks : chunks + 1] + sums[chunks + 1 : chunks + 2]
        share = share + sums[chunks + 2 : chunks + 3]
        exp_others, goal = share[:, 0:1], share[:, LANES // 2 : LANES // 2 + 1]
        exp_total = exp_others + jnp.exp(goal)
        goal_squash = goal * (1.0 / CAP)
        goal_grad = rounded(-exp_others / exp_total * (1.0 - goal_squash * goal_squash))
        grad = sums * (1.0 / exp_total) + goal_row * goal_grad
        grad = grad * final_gain
        x = layer_in[layers]
        scale = norm_scale(x)
        normed = x * scale
        dy = rounded(scale * (grad - normed * (whole(grad * normed) * (1.0 / dim))))

        def layer(step, dy):
            index = layers - 1 - step
            scale = kept[index, 0][0:1]
            hidden_grad = wide_dots(dy, second_wide[index])
            pre_grad = rounded(hidden_grad * kept[index, 1])
            mean = jnp.sum(pre_grad * kept[index, 2], axis=0, keepdims=True)
            act_grad = combine(pre_grad, first_wide[index]) * gain_wide[index]
            back = act_grad - layer_in[index] * (scale * mean * (1.0 / dim))
            return rounded(dy + scale * back)

        dy = lax.fori_loop(0, layers, layer, dy, unroll=2)
        emb_out[...] = dy.reshape(blocks).astype(BF16)

    if_own(backward)
    gather(EMB, emb_out, emb_in)
    take(stat_in, recv_sem.at[STAT])
    tile = lax.fori_loop(
        0, devices // 2, lambda n, acc: acc + stat_in[n], jnp.zeros((2, LANES), F32), unroll=8
    )

    def column_of(kind):
        return jnp.broadcast_to(
            jnp.sum(jnp.where(here, tile[kind : kind + 1], 0.0), axis=1, keepdims=True),
            (count_half, LANES),
        )

    exp_others, goal = column_of(0), column_of(1)
    exp_total = exp_others + jnp.exp(goal)
    stat_sum[side] = tile
    stat_mate = pair_copy(STAT_MATE, stat_sum.at[side], stat_sum.at[side])
    stat_mate.start()
    score_grad = ((powers / both(exp_total) - jnp.where(mask, 1.0, 0.0)) * slope).astype(BF16)
    left_ref[my_rows, :] = score_grad[:, :rows_dev]
    score_out[...] = score_grad[:, rows_dev:]
    score_mate = pair_copy(SCORE_MATE, score_out, score_in)
    score_mate.start()
    head_mate.wait_recv()
    unpack(head_in.at[1 - side], 0, mate_rows)
    stat_mate.wait_recv()
    one = lax.broadcasted_iota(jnp.int32, (1, LANES), 1)
    for b in range(batches):
        for w in range(width):
            k = b * width + w
            sums = stat_sum[k % 2]
            losses = jnp.log(sums[0:1] + jnp.exp(sums[1:2])) - sums[1:2]
            loss_ref[b : b + 1, w : w + 1] = jnp.sum(
                jnp.where(one == rep * own_half + k // 2, losses, 0.0), axis=1, keepdims=True
            )
    score_mate.wait_recv()
    left_ref[mate_rows, :] = score_in[...]
    saves = [
        pltpu.make_async_copy(loss_ref, loss_hbm, recv_sem.at[OUT + 2]),
    ]
    for save in saves:
        save.start()

    take(emb_in.at[side], recv_sem.at[EMB])
    emb_mate = pair_copy(EMB_MATE, emb_in.at[side], emb_in.at[side])
    emb_mate.start()

    unpack(emb_in.at[side], 1, my_rows)
    emb_mate.wait_recv()
    unpack(emb_in.at[1 - side], 1, mate_rows)

    for move in (table_mate, head_mate, stat_mate, score_mate, emb_mate):
        move.wait_send()
    take(idbuf.at[pl.ds(0, replicas - 1)], send_sem.at[IDS])
    for c in range(2):
        take(packed.at[c, 0, 0], send_sem.at[MATE + c])
        if half > 1:
            take(packed.at[c, 0, pl.ds(0, half - 1)], send_sem.at[ACROSS + c])
            take(packed.at[c, 0, pl.ds(0, half - 1)], send_sem.at[RELAY + c])
    take(stat_in.at[pl.ds(0, devices // 2 - 1)], send_sem.at[STAT])
    sent = ((LOOK, look_out), (GOAL, goal_out), (GRAD, grad_out))

    def owned():
        for phase, out in sent:
            take(out.at[pl.ds(0, count_half - 1)], send_sem.at[phase])
        take(look_in.at[pl.ds(0, devices // 2 - 1)], send_sem.at[HEAD])
        take(grad_in.at[pl.ds(0, devices // 2 - 1)], send_sem.at[EMB])

    if_own(owned)
    if not all_own:

        @pl.when(jnp.logical_not(own))
        def _():
            for phase, out in sent:
                take(out, send_sem.at[phase])

    for save in saves:
        save.wait()


def table_kernel(loss_in, left_ref, right_ref, loss_out, out_hbm, right, out, sem, out_sem):
    tokens = right_ref.shape[1]
    steps = out_sem.shape[0]
    rows = out.shape[0] // steps
    moves = [pltpu.make_async_copy(loss_in, loss_out, sem)]
    moves[0].start()
    right[pl.ds(0, tokens), :] = right_ref[0]
    right[pl.ds(tokens, tokens), :] = right_ref[1]
    right[pl.ds(2 * tokens, tokens), :] = right_ref[1]
    across = left_ref[...].astype(F32).T.astype(BF16)
    for i in range(steps):
        at = pl.ds(i * rows, rows)
        out[at, :] = jnp.dot(
            across[i * rows : (i + 1) * rows], right[...], preferred_element_type=F32
        ).astype(BF16)
        save = pltpu.make_async_copy(out.at[at], out_hbm.at[at], out_sem.at[i])
        save.start()
        moves.append(save)
    for move in moves:
        move.wait()


def per_device(token_ids, target_ids, table, norm_gain, w_in, w_out, final_gain):
    sections, replicas = lax.axis_size("section"), lax.axis_size("dp")
    batches, width = token_ids.shape
    rows_dev, dim = table.shape
    rank = w_in.shape[2]
    per_dp = batches * width
    tokens = replicas * per_dp
    devices = sections * replicas
    chunks = dim // LANES
    pad = (chunks + 7) // 8 * 8
    assert per_dp <= sections and tokens % 32 == 0
    assert chunks % 2 == 0 and rows_dev % LANES == 0
    assert per_dp % 2 == 0 and sections % 2 == 0
    assert tokens <= LANES and pad >= chunks + 3
    block = (pad // 8, 8, LANES)
    vmem = pl.BlockSpec(memory_space=pltpu.VMEM)
    hbm = pl.BlockSpec(memory_space=pltpu.HBM)
    inputs = (token_ids, target_ids, table, norm_gain[:, 0], final_gain, w_in, w_out)
    token_loss, left, right = pl.pallas_call(
        functools.partial(cascade, sections, replicas, per_dp, pad, rank),
        out_shape=(
            jax.ShapeDtypeStruct((batches, width), F32),
            pltpu.VMEM((3 * tokens, rows_dev), BF16),
            pltpu.VMEM((2, tokens, dim), BF16),
        ),
        in_specs=[hbm] * 7,
        out_specs=(hbm, vmem, vmem),
        scratch_shapes=[
            pltpu.VMEM((batches, width), jnp.int32),
            pltpu.VMEM((batches, width), jnp.int32),
            pltpu.VMEM((2, dim), BF16),
            pltpu.VMEM((dim,), BF16),
            pltpu.VMEM((2, 1, rank, dim), BF16),
            pltpu.VMEM((2, 1, rank, dim), BF16),
            pltpu.VMEM((batches, width), F32),
            pltpu.VMEM((2 * per_dp, LANES), jnp.int32),
            pltpu.VMEM((replicas, 2 * per_dp, LANES), jnp.int32),
            pltpu.VMEM((2, tokens, LANES), jnp.int32),
            pltpu.VMEM((2, 2, sections // 2, 2 * rank + 1) + block, BF16),
            pltpu.VMEM((2 * sections, pad, LANES), F32),
            pltpu.VMEM((2 * sections, rank, pad, LANES), F32),
            pltpu.VMEM((2 * sections, rank, pad, LANES), F32),
            pltpu.VMEM((max(tokens // 2, rank) * pad, LANES), F32),
            pltpu.VMEM((pad, LANES), F32),
            pltpu.VMEM((tokens // 2,) + block, BF16),
            pltpu.VMEM((devices // 2,) + block, BF16),
            pltpu.VMEM((tokens // 2,) + block, BF16),
            pltpu.VMEM((devices // 2,) + block, BF16),
            pltpu.VMEM((2 * sections + 1, pad, LANES), F32),
            pltpu.VMEM((2 * sections, 3, rank, LANES), F32),
            pltpu.VMEM(block, BF16),
            pltpu.VMEM((2, tokens // 2) + block, BF16),
            pltpu.VMEM((2, LANES), F32),
            pltpu.VMEM((devices // 2, 2, LANES), F32),
            pltpu.VMEM((2, 2, LANES), F32),
            pltpu.VMEM((tokens // 2, rows_dev), BF16),
            pltpu.VMEM((tokens // 2, rows_dev), BF16),
            pltpu.VMEM((tokens // 2,) + block, BF16),
            pltpu.VMEM((devices // 2,) + block, BF16),
            pltpu.VMEM(block, BF16),
            pltpu.VMEM((2, tokens // 2) + block, BF16),
            pltpu.VMEM((2 * rows_dev, dim), BF16),
            pltpu.SemaphoreType.DMA((SEMS,)),
            pltpu.SemaphoreType.DMA((SEMS,)),
        ],
        compiler_params=pltpu.CompilerParams(
            collective_id=0, has_side_effects=True, vmem_limit_bytes=48000000
        ),
        name="cascade",
    )(*[pltpu.with_memory_space_constraint(value, pltpu.HBM) for value in inputs])
    return pl.pallas_call(
        table_kernel,
        out_shape=(
            jax.ShapeDtypeStruct((batches, width), F32),
            jax.ShapeDtypeStruct((rows_dev, dim), BF16),
        ),
        in_specs=[hbm, vmem, vmem],
        out_specs=(hbm, hbm),
        scratch_shapes=[
            pltpu.VMEM((3 * tokens, dim), BF16),
            pltpu.VMEM((rows_dev, dim), BF16),
            pltpu.SemaphoreType.DMA,
            pltpu.SemaphoreType.DMA((4,)),
        ],
        compiler_params=pltpu.CompilerParams(vmem_limit_bytes=16000000),
        name="table_grad",
    )(token_loss, left, right)


def solution(mesh):
    return jax.shard_map(
        per_device,
        mesh=mesh,
        in_specs=(
            P(None, "dp"),
            P(None, "dp"),
            P(("section", "dp"), None),
            P(None, "section", None),
            P(None, "section", None, None),
            P(None, "section", None, None),
            P(),
        ),
        out_specs=(P(None, "dp"), P(("section", "dp"), None)),
        check_vma=False,
    )
```
